128 devices in a mesh: seq: 16 (over y, z), head: 8 (over x, core).
Axes of the slice: x: 4, y: 4, z: 4, core: 2. Of those that a mesh axis runs over, the one named last changes fastest.
Arguments:
- queries: bfloat16 [4096, 128, 576], P('seq', 'head'), may hold values from -6 to 6
- lse: float32 [4096, 128], P('seq', 'head'), may hold values from 8 to 11
- latent: bfloat16 [1024, 128, 576], P('seq'), may hold values from -6 to 6
- index_keys: bfloat16 [1024, 128, 128], P('seq'), may hold values from -6 to 6
- index_queries: bfloat16 [4096, 64, 128], P('seq', 'head'), may hold values from -6 to 6
- index_weights: float32 [4096, 64], P('seq', 'head'), may hold values from 0.03 to 0.3
- block_lists: int32 [32, 16], P('seq'), may hold values from 0 to 1023, as said below
- block_place: int32 [1024], replicated, may hold values from 0 to 1023, as said below
Outputs:
- grad_index_queries: float32 [4096, 64, 128], P('seq', 'head')
- grad_index_weights: float32 [4096, 64], P('seq', 'head')
- grad_index_keys: float32 [1024, 128, 128], P('seq', 'head')
The draws below stay inside these ranges and needn't reach their ends.
Inputs may be any that keep to these rules, and one draw needn't show every extreme that they name: block_place is a permutation of the 1024 pages; page p lies on index p // 64 of seq, and each aligned run of 16 logical blocks (blocks r * 16 to r * 16 + 15) has its pages on 16 different indices of seq. `block_lists`: row g lists 16 different logical blocks, each below 32 * (g + 1). The row is made of 16 runs of 1 entries; the entries of run k are blocks whose pages lie on index k of seq.
All inputs are finite; a program needn't handle non-finite values.
Results may differ from the reference program's by a relative error of at most 0.0029.
Values may be sent and summed in bfloat16 or wider, within the bound.
No kernel may reach another device: no remote copies, remote signals or barrier semaphores. Data moves between devices by JAX's collectives and lax.ppermute only.
A program may use at most 128 MiB of HBM per device.

```python
import math
import jax
import jax.numpy as jnp
from jax import lax

LAT = 576
HEADS = 128
IDXH = 64
IDXD = 128
BLOCK = 128
SEL = 16
QBLK = 128
KREG = 32
QB_DEV = 2
NB = 1024
QB = 32
Q = 4096
N_SEQ = 16


def page_layout(key):
    base = jax.random.fold_in(key, 7301)
    rounds = KREG * QB_DEV
    round_keys = jax.random.split(jax.random.fold_in(base, 1), rounds)
    owners = jax.vmap(lambda subkey: jax.random.permutation(subkey, N_SEQ))(round_keys).astype(jnp.int32)
    owner_keys = jax.random.split(jax.random.fold_in(base, 2), N_SEQ)
    orders = jax.vmap(lambda subkey: jax.random.permutation(subkey, rounds))(owner_keys).astype(jnp.int32)
    round_grid = jnp.broadcast_to(jnp.arange(rounds, dtype=jnp.int32)[:, None], owners.shape)
    slot_grid = orders[owners, round_grid]
    placed = (owners * rounds + slot_grid).reshape(-1).astype(jnp.int32)
    positions = jnp.argsort(owners, axis=1).astype(jnp.int32)
    return (placed, positions)


def select_blocks(key):
    placed, positions = page_layout(key)
    rounds = KREG * QB_DEV
    groups = QB_DEV * N_SEQ
    per_owner = SEL // N_SEQ
    visible = KREG * (jnp.arange(groups, dtype=jnp.int32) + 1) // N_SEQ
    round_ids = jnp.arange(rounds, dtype=jnp.int32)
    ages = visible[:, None] - 1 - round_ids[None, :]
    draws = jax.random.randint(jax.random.fold_in(key, 7302), (groups, N_SEQ, rounds), 1, 4096, dtype=jnp.int32)
    weighted = draws * 64 // (jnp.maximum(ages, 0)[:, None, :] + 1)
    ranked = jnp.where((ages >= 0)[:, None, :], weighted * rounds + round_ids[None, None, :], -1 - round_ids[None, None, :])
    chosen = lax.top_k(ranked, per_owner)[1].astype(jnp.int32)
    owner_ids = jnp.broadcast_to(jnp.arange(N_SEQ, dtype=jnp.int32)[None, :, None], chosen.shape)
    blocks = chosen * N_SEQ + positions[chosen, owner_ids]
    return blocks.reshape(groups, SEL).astype(jnp.int32)


def key_base(key):
    values = jax.random.normal(jax.random.fold_in(key, 7303), (KREG * QB_DEV * N_SEQ, BLOCK, IDXD), jnp.float32)
    return jnp.clip(values, -6.0, 6.0)


def draw_block_place(key, part):
    return page_layout(key)[0]


def draw_block_lists(key, part):
    return select_blocks(key)


def draw_index_keys(key, part):
    keys_all = key_base(key)
    return keys_all.astype(jnp.bfloat16)


def draw_index_queries(key, part):
    total = QB_DEV * N_SEQ * QBLK
    values = 0.1 * jax.random.normal(jax.random.fold_in(key, 7304), (total, IDXH, IDXD), jnp.float32)
    values = jnp.clip(values, -0.6, 0.6)
    return values.astype(jnp.bfloat16)


def steps_of(rng, shape, cuts, least, top_value):
    loudness = 1.0
    for dim, shards_of in cuts:
        steps = jax.random.uniform(jax.random.fold_in(jax.random.fold_in(rng, 6), dim), (shards_of,), jnp.float32, least / len(cuts), top_value / len(cuts))
        loudness = loudness * jnp.repeat(jnp.exp(steps), shape[dim] // shards_of).reshape((-1,) + (1,) * (len(shape) - 1 - dim))
    return loudness


def normal_values(rng, extent, deviation, limit, cuts=(), kind=jnp.bfloat16):
    loudness = steps_of(rng, extent, cuts, -0.22, 0.18) if cuts else 1.0
    result = jax.random.normal(rng, extent, jnp.float32) * deviation * loudness
    return jnp.minimum(jnp.maximum(result, -limit), limit).astype(kind)


def setup_inputs(seed: int = 0) -> dict:
    arg_keys = jax.random.split(jax.random.key(seed), 9)
    queries = normal_values(arg_keys[0], (Q, HEADS, LAT), 1.0, 6.0, ((0, 16), (1, 8)))
    lse = jnp.clip(8.0 + 3.0 * jax.random.uniform(arg_keys[1], (Q, HEADS), jnp.float32) ** steps_of(arg_keys[1], (Q, HEADS), ((0, 16), (1, 8)), -0.2, 0.2), 8.0, 11.0)
    latent = normal_values(arg_keys[2], (NB, BLOCK, LAT), 1.0, 6.0, ((0, 16),))
    index_keys = draw_index_keys(jax.random.fold_in(arg_keys[8], 71), 0)
    index_queries = draw_index_queries(jax.random.fold_in(arg_keys[8], 71), 0)
    index_weights = jnp.clip(jnp.exp(math.log(0.3) - 2.3025852 * jax.random.uniform(arg_keys[5], (Q, IDXH), jnp.float32) ** steps_of(arg_keys[5], (Q, IDXH), ((0, 16), (1, 8)), -0.2, 0.2)), 0.03, 0.3)
    block_lists = draw_block_lists(jax.random.fold_in(arg_keys[8], 71), 0)
    block_place = draw_block_place(jax.random.fold_in(arg_keys[8], 71), 0)
    return {"queries": queries, "lse": lse, "latent": latent, "index_keys": index_keys, "index_queries": index_queries, "index_weights": index_weights, "block_lists": block_lists, "block_place": block_place}


softmax_scale = 192.0 ** -0.5
loss_scale = 2048.0


def reference(queries, lse, latent, index_keys, index_queries, index_weights, block_lists, block_place):
    def step(grad_keys, block_index):
        pages = block_place[block_lists[block_index]]
        key_rows = latent[pages].reshape(SEL * BLOCK, LAT).astype(jnp.float32)
        index_rows = index_keys[pages].reshape(SEL * BLOCK, IDXD).astype(jnp.float32)
        first = block_index * QBLK
        query_rows = lax.dynamic_slice_in_dim(queries, first, QBLK, 0).astype(jnp.float32)
        lse_rows = lax.dynamic_slice_in_dim(lse, first, QBLK, 0)
        probe_rows = lax.dynamic_slice_in_dim(index_queries, first, QBLK, 0).astype(jnp.float32)
        head_weights = lax.dynamic_slice_in_dim(index_weights, first, QBLK, 0)
        scores = jnp.einsum("qhd,kd->qhk", query_rows, key_rows) * softmax_scale
        teacher = jnp.sum(jnp.exp(scores - lse_rows[:, :, None]), axis=1)
        target = teacher / jnp.sum(teacher, axis=1, keepdims=True)
        raw_scores = jnp.einsum("qhd,kd->qhk", probe_rows, index_rows)
        active = jnp.maximum(raw_scores, 0.0)
        score = jnp.sum(head_weights[:, :, None] * active, axis=1)
        probs = jax.nn.softmax(score, axis=-1)
        grad_score = loss_scale * (probs - target)
        grad_weight = jnp.sum(grad_score[:, None, :] * active, axis=2)
        grad_raw = (grad_score[:, None, :] * head_weights[:, :, None] * (raw_scores > 0).astype(jnp.float32)).astype(jnp.bfloat16)
        grad_raw = lax.optimization_barrier(grad_raw).astype(jnp.float32)
        grad_query = jnp.einsum("qhk,kd->qhd", grad_raw, index_rows)
        key_grad = jnp.einsum("qhk,qhd->kd", grad_raw, probe_rows)
        grad_keys = grad_keys.at[pages].add(key_grad.reshape(SEL, BLOCK, IDXD))
        return grad_keys, (grad_query, grad_weight)

    initial = jnp.zeros((NB, BLOCK, IDXD), jnp.float32)
    grad_keys, (grad_queries, grad_weights) = lax.scan(step, initial, jnp.arange(QB, dtype=jnp.int32))
    return grad_queries.reshape(Q, IDXH, IDXD), grad_weights.reshape(Q, IDXH), grad_keys
```

```python
import functools
import math

import jax
import jax.numpy as jnp
from jax import lax
from jax.experimental import pallas as pl
from jax.experimental.pallas import tpu as pltpu
from jax.sharding import PartitionSpec as P

BLOCK = 128
SEL = 16
QBLK = 128
LAT = 576
IDXD = 128
IDXH = 64
QPART = 32
WIDE = LAT + IDXD

f32 = jnp.float32
bf16 = jnp.bfloat16

LOG2E = math.log2(math.e)
softmax_scale = 192.0 ** (-0.5)
loss_scale = 2048.0

NT = (((1,), (1,)), ((), ()))
NN = (((1,), (0,)), ((), ()))


def dot_nt(a, b):
    return lax.dot_general(a, b, NT, preferred_element_type=f32)


def dot_nn(a, b):
    return lax.dot_general(a, b, NN, preferred_element_type=f32)


def pack_body(slots_ref, keys_ref, lat_ref, out_ref):
    out_ref[0, :, :IDXD] = keys_ref[0]
    out_ref[0, :, IDXD:] = lat_ref[0]


def pack_pages(slots, index_keys, latent):
    n = slots.shape[0]
    return pl.pallas_call(
        pack_body,
        out_shape=jax.ShapeDtypeStruct((n, BLOCK, WIDE), bf16),
        grid_spec=pltpu.PrefetchScalarGridSpec(
            num_scalar_prefetch=1,
            grid=(n,),
            in_specs=[
                pl.BlockSpec((1, BLOCK, IDXD), lambda i, s: (s[i], 0, 0)),
                pl.BlockSpec((1, BLOCK, LAT), lambda i, s: (s[i], 0, 0)),
            ],
            out_specs=pl.BlockSpec((1, BLOCK, WIDE), lambda i, s: (i, 0, 0)),
        ),
        cost_estimate=pl.CostEstimate(flops=0, bytes_accessed=n * BLOCK * WIDE * 4, transcendentals=0),
        name="pack_pages",
    )(slots, index_keys, latent)


HG = 8


def teacher_body(qa_ref, qb_ref, la_ref, lb_ref, kj_ref, out_ref):
    keys = kj_ref[:, :, IDXD:].reshape(-1, LAT)
    acc = None
    for q_ref, l_ref in ((qa_ref, la_ref), (qb_ref, lb_ref)):
        heads = q_ref.shape[0]
        for g in range(heads // HG):
            rows = q_ref[g * HG : (g + 1) * HG].reshape(HG * QBLK, LAT)
            s = dot_nt(rows, keys)
            for k in range(HG):
                h = g * HG + k
                col = l_ref[:, h : h + 1] * LOG2E
                part = jnp.exp2(s[k * QBLK : (k + 1) * QBLK] * (softmax_scale * LOG2E) - col)
                acc = part if acc is None else acc + part
    out_ref[...] = acc


def teacher_terms(qa, qb, la, lb, kj):
    tile = 2
    n = kj.shape[0]
    whole = lambda a: pl.BlockSpec(a.shape, lambda i: (0,) * a.ndim)
    return pl.pallas_call(
        teacher_body,
        out_shape=jax.ShapeDtypeStruct((QBLK, n * BLOCK), f32),
        grid=(n // tile,),
        in_specs=[whole(qa), whole(qb), whole(la), whole(lb), pl.BlockSpec((tile, BLOCK, WIDE), lambda i: (i, 0, 0))],
        out_specs=pl.BlockSpec((QBLK, tile * BLOCK), lambda i: (0, i)),
        cost_estimate=pl.CostEstimate(flops=2 * 32 * QBLK * n * BLOCK * LAT, bytes_accessed=12 << 20, transcendentals=32 * QBLK * n * BLOCK),
        name="teacher_terms",
    )(qa, qb, la, lb, kj)


def weights_of(pack_ref, e):
    src, i = divmod(e, 8)
    rows = pack_ref[src, 8 * QPART :, :].astype(f32)
    return rows[:, i : i + 1] + rows[:, 8 + i : 9 + i] + rows[:, 16 + i : 17 + i]


def score_body(iq_ref, kj_ref, out_ref):
    keys = kj_ref[:, :, :IDXD].reshape(-1, IDXD)
    acc = None
    for src in range(8):
        raw = dot_nt(iq_ref[src, : 8 * QPART, :], keys)
        for i in range(8):
            part = jnp.maximum(raw[i * QPART : (i + 1) * QPART], 0.0) * weights_of(iq_ref, src * 8 + i)
            acc = part if acc is None else acc + part
    out_ref[...] = acc


def scores(iq, kj):
    tile = 4
    n = kj.shape[0]
    return pl.pallas_call(
        score_body,
        out_shape=jax.ShapeDtypeStruct((QPART, n * BLOCK), f32),
        grid=(n // tile,),
        in_specs=[pl.BlockSpec(iq.shape, lambda i: (0, 0, 0)), pl.BlockSpec((tile, BLOCK, IDXD), lambda i: (i, 0, 0))],
        out_specs=pl.BlockSpec((QPART, tile * BLOCK), lambda i: (0, i)),
        cost_estimate=pl.CostEstimate(flops=2 * IDXH * QPART * n * BLOCK * IDXD, bytes_accessed=2 << 20, transcendentals=0),
        name="scores",
    )(iq, kj)


def backward_body(own_ref, t1_ref, t2_ref, t3_ref, score_ref, iq_ref, iqt_ref, kj_ref, gk_ref, gq_ref, grad_ref, gw_ref):
    step = pl.program_id(0)
    span = gk_ref.shape[0]

    @pl.when(step == 0)
    def _():
        teacher = own_ref[...] + t1_ref[...].astype(f32) + t2_ref[...].astype(f32) + t3_ref[...].astype(f32)
        target = teacher / jnp.sum(teacher, axis=1, keepdims=True)
        score = score_ref[...]
        e = jnp.exp(score - jnp.max(score, axis=1, keepdims=True))
        probs = e / jnp.sum(e, axis=1, keepdims=True)
        grad_ref[...] = loss_scale * (probs - target)
        gq_ref[...] = jnp.zeros_like(gq_ref)
        gw_ref[...] = jnp.zeros_like(gw_ref)

    keys = kj_ref[:, :, :IDXD].reshape(-1, IDXD)
    grad = grad_ref[:, pl.ds(pl.multiple_of(step * span, span), span)]
    gkt = None
    lane = lax.broadcasted_iota(jnp.int32, (QPART, IDXD), 1)
    for src in range(8):
        raw = dot_nt(iq_ref[src, : 8 * QPART, :], keys)
        parts = []
        gws = jnp.zeros((QPART, IDXD), f32)
        for i in range(8):
            r = raw[i * QPART : (i + 1) * QPART]
            gw = grad * jnp.maximum(r, 0.0)
            gws = gws + jnp.where(lane == i, jnp.sum(gw, axis=1, keepdims=True), 0.0)
            w = weights_of(iq_ref, src * 8 + i)
            parts.append(jnp.where(r > 0.0, grad * w, 0.0).astype(bf16))
        gr = jnp.concatenate(parts, axis=0)
        gq_ref[src, : 8 * QPART, :] += dot_nn(gr, keys)
        gq_ref[src, 8 * QPART :, :] += gws
        piece = dot_nn(iqt_ref[:, src * 8 * QPART : (src + 1) * 8 * QPART], gr)
        gkt = piece if gkt is None else gkt + piece
    gk_ref[...] = gkt.T.astype(gk_ref.dtype)


def backward(own, t1, t2, t3, score, iq, iqt, kj):
    tile = 4
    n = kj.shape[0]
    whole = lambda a: pl.BlockSpec(a.shape, lambda i: (0,) * a.ndim)
    return pl.pallas_call(
        backward_body,
        out_shape=(
            jax.ShapeDtypeStruct((n * BLOCK, IDXD), bf16),
            jax.ShapeDtypeStruct((8, 9 * QPART, IDXD), f32),
        ),
        grid=(n // tile,),
        in_specs=[whole(a) for a in (own, t1, t2, t3, score, iq, iqt)] + [pl.BlockSpec((tile, BLOCK, IDXD), lambda i: (i, 0, 0))],
        out_specs=(
            pl.BlockSpec((tile * BLOCK, IDXD), lambda i: (i, 0)),
            pl.BlockSpec((8, 9 * QPART, IDXD), lambda i: (0, 0, 0)),
        ),
        scratch_shapes=[pltpu.VMEM((QPART, n * BLOCK), f32), pltpu.VMEM((8, 128), f32)],
        cost_estimate=pl.CostEstimate(flops=6 * IDXH * QPART * n * BLOCK * IDXD, bytes_accessed=4 << 20, transcendentals=0),
        name="backward",
    )(own, t1, t2, t3, score, iq, iqt, kj)


def split3(a):
    hi = lax.reduce_precision(a, 8, 7)
    mid = lax.reduce_precision(a - hi, 8, 7)
    lo = a - hi - mid
    return [hi.astype(bf16), mid.astype(bf16), lo.astype(bf16)]


def shards(queries, lse, latent, index_keys, index_queries, index_weights, block_lists, block_place):
    page_count = latent.shape[0]
    head = lax.axis_index("head")
    core = head % 2
    quarter = head // 2
    partner = [(h, h ^ 1) for h in range(8)]

    pages = jnp.take(block_place, block_lists, axis=0) % page_count
    wanted = lax.all_to_all(pages.T.reshape(SEL, 1, 2), "seq", split_axis=0, concat_axis=0, tiled=True)
    wanted = wanted.reshape(SEL, 2)

    heads = queries.shape[1]
    by_head = queries.reshape(2, QBLK, heads, LAT).transpose(0, 2, 1, 3)
    qa = lax.dynamic_index_in_dim(by_head, core, 0, keepdims=False)
    qb = lax.ppermute(lax.dynamic_index_in_dim(by_head, 1 - core, 0, keepdims=False), "head", partner)
    lses = lse.reshape(2, QBLK, heads)
    la = lax.dynamic_index_in_dim(lses, core, 0, keepdims=False)
    lb = lax.ppermute(lax.dynamic_index_in_dim(lses, 1 - core, 0, keepdims=False), "head", partner)

    ih = index_queries.shape[1]
    iq = index_queries.reshape(2, 4, QPART, ih, IDXD).transpose(1, 0, 3, 2, 4).reshape(8, ih * QPART, IDXD)
    iw = index_weights.reshape(2, 4, QPART, ih).transpose(1, 0, 2, 3).reshape(8, QPART, ih)
    iw = jnp.concatenate(split3(iw) + [jnp.zeros((8, QPART, IDXD - 3 * ih), bf16)], axis=2)
    iq = lax.all_to_all(jnp.concatenate([iq, iw], axis=1), "head", split_axis=0, concat_axis=0, tiled=True)
    iqt = iq[:, : ih * QPART].reshape(8 * ih * QPART, IDXD).T

    mine = lax.dynamic_index_in_dim(wanted, core, 1, keepdims=False)
    kj = lax.all_to_all(pack_pages(mine, index_keys, latent), "seq", split_axis=0, concat_axis=0, tiled=True)

    score = scores(iq, kj)
    teacher = teacher_terms(qa, qb, la, lb, kj)

    quarters = teacher.reshape(4, QPART, SEL * BLOCK)
    moved = []
    for d in (2, 1, 3):
        ring = [(2 * x + c, 2 * ((x + d) % 4) + c) for x in range(4) for c in range(2)]
        part = lax.dynamic_index_in_dim(quarters, (quarter + d) % 4, 0, keepdims=False)
        moved.append(lax.ppermute(part.astype(bf16), "head", ring))
    own = lax.dynamic_index_in_dim(quarters, quarter, 0, keepdims=False)

    gk, gq = backward(own, *moved, score, iq, iqt, kj)

    gk = lax.all_to_all(gk.reshape(128, 16, IDXD), ("seq", "head"), split_axis=0, concat_axis=0, tiled=True)
    gq = lax.all_to_all(gq, "head", split_axis=0, concat_axis=0, tiled=True)

    slots = jnp.broadcast_to(wanted[:, None, :], (SEL, 4, 2)).reshape(128)
    onehot = (jnp.arange(page_count, dtype=jnp.int32)[:, None] == slots[None, :]).astype(bf16)
    grad_keys = jnp.dot(onehot, gk.reshape(128, 16 * IDXD), preferred_element_type=f32).reshape(page_count, 16, IDXD)

    gw = gq[:, 8 * QPART :, :ih].reshape(4, 2, QPART, ih).transpose(1, 0, 2, 3).reshape(2 * QBLK, ih)
    gq = gq[:, : 8 * QPART].reshape(4, 2, ih, QPART, IDXD).transpose(1, 0, 3, 2, 4).reshape(2 * QBLK, ih, IDXD)
    return gq, gw, grad_keys


def solution(mesh):
    return jax.shard_map(
        shards,
        mesh=mesh,
        in_specs=(
            P("seq", "head", None),
            P("seq", "head"),
            P("seq", None, None),
            P("seq", None, None),
            P("seq", "head", None),
            P("seq", "head"),
            P("seq", None),
            P(),
        ),
        out_specs=(P("seq", "head", None), P("seq", "head"), P("seq", "head", None)),
        check_vma=False,
    )
```

```python
import math

import jax
import jax.numpy as jnp
from jax import lax
from jax.experimental import pallas as pl
from jax.experimental.pallas import tpu as pltpu
from jax.sharding import PartitionSpec as P

BLOCK = 128
SEL = 16
QBLK = 128
LAT = 576
LATP = 640
IDXD = 128
IDXH = 64
QPART = 32
ROWS = LAT + IDXD

f32 = jnp.float32
bf16 = jnp.bfloat16

LOG2E = math.log2(math.e)
softmax_scale = 192.0 ** (-0.5)
loss_scale = 2048.0


def dot(a, b):
    return lax.dot_general(a, b, (((1,), (0,)), ((), ())), preferred_element_type=f32)


def dot_nt(a, b):
    return lax.dot_general(a, b, (((1,), (1,)), ((), ())), preferred_element_type=f32)


def whole(a):
    return pl.BlockSpec(a.shape, lambda *i: (0,) * a.ndim)


def pack_body(slots_ref, lat_ref, key_ref, out_ref, sems):
    copies = []
    for i in range(SEL):
        copies.append(pltpu.make_async_copy(lat_ref.at[slots_ref[i]], out_ref.at[i, :LAT, :], sems.at[2 * i]))
        copies.append(pltpu.make_async_copy(key_ref.at[slots_ref[i]], out_ref.at[i, LAT:, :], sems.at[2 * i + 1]))
    for c in copies:
        c.start()
    for c in copies:
        c.wait()


def pack_pages(slots, lat, keys):
    return pl.pallas_call(
        pack_body,
        out_shape=jax.ShapeDtypeStruct((SEL, ROWS, BLOCK), bf16),
        in_specs=[
            pl.BlockSpec(memory_space=pltpu.SMEM),
            pl.BlockSpec(memory_space=pl.ANY),
            pl.BlockSpec(memory_space=pl.ANY),
        ],
        out_specs=pl.BlockSpec(memory_space=pltpu.VMEM),
        scratch_shapes=[pltpu.SemaphoreType.DMA((2 * SEL,))],
        cost_estimate=pl.CostEstimate(flops=0, bytes_accessed=6 << 20, transcendentals=0),
        name="pack_pages",
    )(slots, lat, keys)


def flip_body(core_ref, qo_ref, qs_ref, lo_ref, ls_ref, own_ref, send_ref, lown_ref, lsend_ref):
    for q_ref, o_ref in ((qo_ref, own_ref), (qs_ref, send_ref)):
        for h in range(q_ref.shape[0]):
            o_ref[h, :, :LAT] = q_ref[h].T
            o_ref[h, :, LAT:] = jnp.zeros((QBLK, LATP - LAT), bf16)

    @pl.when(pl.program_id(0) == 0)
    def _():
        for l_ref, o_ref in ((lo_ref, lown_ref), (ls_ref, lsend_ref)):
            o_ref[...] = jnp.zeros_like(o_ref)
            o_ref[:, : l_ref.shape[0]] = l_ref[...].T * LOG2E


def flip_queries(core, qt, lt):
    heads = qt.shape[0]
    hb = 4
    qspec = lambda own: pl.BlockSpec((hb, LAT, QBLK), lambda i, c: (i, 0, c[0] if own else 1 - c[0]))
    lspec = lambda own: pl.BlockSpec((heads, QBLK), lambda i, c: (0, c[0] if own else 1 - c[0]))
    oq = jax.ShapeDtypeStruct((heads, QBLK, LATP), bf16)
    ol = jax.ShapeDtypeStruct((QBLK, 128), f32)
    oqs = pl.BlockSpec((hb, QBLK, LATP), lambda i, c: (i, 0, 0))
    ols = pl.BlockSpec((QBLK, 128), lambda i, c: (0, 0))
    return pl.pallas_call(
        flip_body,
        out_shape=(oq, oq, ol, ol),
        grid_spec=pltpu.PrefetchScalarGridSpec(
            num_scalar_prefetch=1,
            grid=(heads // hb,),
            in_specs=[qspec(True), qspec(False), lspec(True), lspec(False)],
            out_specs=(oqs, oqs, ols, ols),
        ),
        cost_estimate=pl.CostEstimate(flops=0, bytes_accessed=24 << 20, transcendentals=0),
        name="flip_queries",
    )(core, qt, qt, lt, lt)


HG = 16
PT = 4


def teacher_body(quarter_ref, qa_ref, qb_ref, la_ref, lb_ref, kj_ref, out_ref):
    keys = jnp.concatenate([kj_ref[p, :LATP, :] for p in range(PT)], axis=1)
    acc = None
    for q_ref, l_ref in ((qa_ref, la_ref), (qb_ref, lb_ref)):
        s = dot(q_ref[...].reshape(HG * QPART, LATP), keys)
        for h in range(HG):
            part = jnp.exp2(s[h * QPART : (h + 1) * QPART] * (softmax_scale * LOG2E) - l_ref[:, h : h + 1])
            acc = part if acc is None else acc + part
    out_ref[...] = acc.astype(out_ref.dtype)


def teacher_terms(quarter, qa, qb, la, lb, kj, dtype):
    n = kj.shape[0]
    qspec = pl.BlockSpec((HG, QPART, LATP), lambda i, q: (0, q[0], 0))
    lspec = pl.BlockSpec((QPART, 128), lambda i, q: (q[0], 0))
    return pl.pallas_call(
        teacher_body,
        out_shape=jax.ShapeDtypeStruct((QPART, n * BLOCK), dtype),
        grid_spec=pltpu.PrefetchScalarGridSpec(
            num_scalar_prefetch=1,
            grid=(n // PT,),
            in_specs=[qspec, qspec, lspec, lspec, pl.BlockSpec((PT, ROWS, BLOCK), lambda i, q: (i, 0, 0))],
            out_specs=pl.BlockSpec((QPART, PT * BLOCK), lambda i, q: (0, i)),
        ),
        cost_estimate=pl.CostEstimate(
            flops=2 * 32 * QPART * n * BLOCK * LAT, bytes_accessed=6 << 20, transcendentals=32 * QPART * n * BLOCK
        ),
        name="teacher_terms",
    )(quarter, qa, qb, la, lb, kj)


PS = 4


def score_body(iq_ref, kj_ref, out_ref, wb_ref):
    @pl.when(pl.program_id(0) == 0)
    def _():
        for src in range(8):
            rows = iq_ref[src, 8 * QPART :, :].astype(f32)
            for i in range(8):
                col = rows[:, i : i + 1] + rows[:, 8 + i : 9 + i] + rows[:, 16 + i : 17 + i]
                wb_ref[src * 8 + i] = jnp.broadcast_to(col, (QPART, 128))

    keys = kj_ref[:, LAT:, :].reshape(-1, IDXD)
    raw = dot_nt(iq_ref[:, : 8 * QPART, :].reshape(IDXH * QPART, IDXD), keys)
    for t in range(PS):
        acc = None
        for e in range(IDXH):
            r = raw[e * QPART : (e + 1) * QPART, t * 128 : (t + 1) * 128]
            part = jnp.maximum(r, 0.0) * wb_ref[e]
            acc = part if acc is None else acc + part
        out_ref[:, t * 128 : (t + 1) * 128] = acc


def scores(iq, kj):
    n = kj.shape[0]
    return pl.pallas_call(
        score_body,
        out_shape=(
            jax.ShapeDtypeStruct((QPART, n * BLOCK), f32),
            jax.ShapeDtypeStruct((IDXH, QPART, 128), f32),
        ),
        grid=(n // PS,),
        in_specs=[whole(iq), pl.BlockSpec((PS, ROWS, BLOCK), lambda i: (i, 0, 0))],
        out_specs=(
            pl.BlockSpec((QPART, PS * BLOCK), lambda i: (0, i)),
            pl.BlockSpec((IDXH, QPART, 128), lambda i: (0, 0, 0)),
        ),
        cost_estimate=pl.CostEstimate(flops=2 * IDXH * QPART * n * BLOCK * IDXD, bytes_accessed=6 << 20, transcendentals=0),
        name="scores",
    )(iq, kj)


PB = 4


def backward_body(own_ref, t1_ref, t2_ref, t3_ref, score_ref, iq_ref, iqt_ref, wb_ref, kj_ref, gk_ref, gq_ref, grad_ref, gr_ref, gw_ref, acc_ref):
    step = pl.program_id(0)
    span = PB * BLOCK

    @pl.when(step == 0)
    def _():
        teacher = own_ref[...] + t1_ref[...].astype(f32) + t2_ref[...].astype(f32) + t3_ref[...].astype(f32)
        target = teacher / jnp.sum(teacher, axis=1, keepdims=True)
        score = score_ref[...]
        e = jnp.exp(score - jnp.max(score, axis=1, keepdims=True))
        probs = e / jnp.sum(e, axis=1, keepdims=True)
        grad_ref[...] = loss_scale * (probs - target)
        acc_ref[...] = jnp.zeros_like(acc_ref)
        gw_ref[...] = jnp.zeros_like(gw_ref)

    keys = kj_ref[:, LAT:, :].reshape(-1, IDXD)
    raw = dot_nt(iq_ref[:, : 8 * QPART, :].reshape(IDXH * QPART, IDXD), keys)
    for e in range(IDXH):
        gsum = gw_ref[e]
        w = wb_ref[e]
        for t in range(PB):
            g = grad_ref[:, pl.ds(pl.multiple_of(step * span + t * 128, 128), 128)]
            r = raw[e * QPART : (e + 1) * QPART, t * 128 : (t + 1) * 128]
            gsum = gsum + g * jnp.maximum(r, 0.0)
            gr_ref[e * QPART : (e + 1) * QPART, t * 128 : (t + 1) * 128] = jnp.where(r > 0.0, g * w, 0.0).astype(bf16)
        gw_ref[e] = gsum
    gr = gr_ref[...]
    gk_ref[...] = dot(iqt_ref[...], gr).T.astype(gk_ref.dtype)
    acc_ref[...] += dot(gr, keys)

    @pl.when(step == pl.num_programs(0) - 1)
    def _():
        lane = lax.broadcasted_iota(jnp.int32, (QPART, 128), 1)
        for src in range(8):
            gq_ref[src, : 8 * QPART, :] = acc_ref[src * 8 * QPART : (src + 1) * 8 * QPART, :].astype(bf16)
            out = jnp.zeros((QPART, 128), f32)
            for i in range(8):
                rest = jnp.sum(gw_ref[src * 8 + i], axis=1, keepdims=True)
                for k in range(3):
                    piece = rest.astype(bf16).astype(f32)
                    out = jnp.where(lane == 8 * k + i, piece, out)
                    rest = rest - piece
            gq_ref[src, 8 * QPART :, :] = out.astype(bf16)


def backward(own, moved, score, iq, iqt, wb, kj):
    n = kj.shape[0]
    fixed = (own, *moved, score, iq, iqt, wb)
    return pl.pallas_call(
        backward_body,
        out_shape=(
            jax.ShapeDtypeStruct((n * BLOCK, IDXD), bf16),
            jax.ShapeDtypeStruct((8, 9 * QPART, IDXD), bf16),
        ),
        grid=(n // PB,),
        in_specs=[whole(a) for a in fixed] + [pl.BlockSpec((PB, ROWS, BLOCK), lambda i: (i, 0, 0))],
        out_specs=(
            pl.BlockSpec((PB * BLOCK, IDXD), lambda i: (i, 0)),
            pl.BlockSpec((8, 9 * QPART, IDXD), lambda i: (0, 0, 0)),
        ),
        scratch_shapes=[
            pltpu.VMEM((QPART, n * BLOCK), f32),
            pltpu.VMEM((IDXH * QPART, PB * BLOCK), bf16),
            pltpu.VMEM((IDXH, QPART, 128), f32),
            pltpu.VMEM((IDXH * QPART, IDXD), f32),
        ],
        cost_estimate=pl.CostEstimate(flops=6 * IDXH * QPART * n * BLOCK * IDXD, bytes_accessed=8 << 20, transcendentals=0),
        name="backward",
    )(*fixed, kj)


def split3(a):
    hi = lax.reduce_precision(a, 8, 7)
    mid = lax.reduce_precision(a - hi, 8, 7)
    lo = a - hi - mid
    return [hi.astype(bf16), mid.astype(bf16), lo.astype(bf16)]


def shards(queries, lse, latent, index_keys, index_queries, index_weights, block_lists, block_place):
    page_count = latent.shape[0]
    head = lax.axis_index("head")
    core = head & 1
    quarter = head >> 1
    partner = [(h, h ^ 1) for h in range(8)]

    pages = block_place.at[block_lists].get(mode="promise_in_bounds") & (page_count - 1)
    wanted = lax.all_to_all(pages.T.reshape(SEL, 1, 2), "seq", split_axis=0, concat_axis=0, tiled=True)
    wanted = wanted.reshape(SEL, 2)

    ih = index_queries.shape[1]
    iq = index_queries.reshape(2, 4, QPART, ih, IDXD).transpose(1, 0, 3, 2, 4).reshape(8, ih * QPART, IDXD)
    iw = index_weights.reshape(2, 4, QPART, ih).transpose(1, 0, 2, 3).reshape(8, QPART, ih)
    iw = jnp.concatenate(split3(iw) + [jnp.zeros((8, QPART, IDXD - 3 * ih), bf16)], axis=2)
    iq = jnp.concatenate([iq, iw], axis=1)

    mine = lax.dynamic_index_in_dim(wanted, core, 1, keepdims=False)
    packed = pack_pages(mine, latent.transpose(0, 2, 1), index_keys)
    packed, iq = lax.optimization_barrier((packed, iq))
    kj = lax.all_to_all(packed, "seq", split_axis=0, concat_axis=0, tiled=True)
    iq = lax.all_to_all(iq, "head", split_axis=0, concat_axis=0, tiled=True)
    iqt = iq[:, : ih * QPART].reshape(8 * ih * QPART, IDXD).T

    qa, qs, la, ls = flip_queries(core.reshape(1), queries.transpose(1, 2, 0), lse.T)
    qb = lax.ppermute(qs, "head", partner)
    lb = lax.ppermute(ls, "head", partner)

    score, wb = scores(iq, kj)

    moved = []
    for d in (2, 1, 3):
        ring = [(2 * x + c, 2 * ((x + d) % 4) + c) for x in range(4) for c in range(2)]
        part = teacher_terms(((quarter + d) & 3).reshape(1), qa, qb, la, lb, kj, bf16)
        moved.append(lax.ppermute(part, "head", ring))
    own = teacher_terms(quarter.reshape(1), qa, qb, la, lb, kj, f32)

    gk, gq = backward(own, moved, score, iq, iqt, wb, kj)

    gk = lax.all_to_all(gk.reshape(128, 16, IDXD), ("seq", "head"), split_axis=0, concat_axis=0, tiled=True)
    gq = lax.all_to_all(gq, "head", split_axis=0, concat_axis=0, tiled=True)

    slots = jnp.broadcast_to(wanted[:, None, :], (SEL, 4, 2)).reshape(128)
    onehot = (jnp.arange(page_count, dtype=jnp.int32)[:, None] == slots[None, :]).astype(bf16)
    grad_keys = jnp.dot(onehot, gk.reshape(128, 16 * IDXD), preferred_element_type=f32).reshape(page_count, 16, IDXD)

    gw = gq[:, 8 * QPART :, : 3 * ih].astype(f32).reshape(4, 2, QPART, 3, ih).sum(axis=3)
    gw = gw.transpose(1, 0, 2, 3).reshape(2 * QBLK, ih)
    gq = gq[:, : 8 * QPART].astype(f32).reshape(4, 2, ih, QPART, IDXD).transpose(1, 0, 3, 2, 4).reshape(2 * QBLK, ih, IDXD)
    return gq, gw, grad_keys


def solution(mesh):
    return jax.shard_map(
        shards,
        mesh=mesh,
        in_specs=(
            P("seq", "head", None),
            P("seq", "head"),
            P("seq", None, None),
            P("seq", None, None),
            P("seq", "head", None),
            P("seq", "head"),
            P("seq", None),
            P(),
        ),
        out_specs=(P("seq", "head", None), P("seq", "head"), P("seq", "head", None)),
        check_vma=False,
    )
```

```python
import math

import jax
import jax.numpy as jnp
from jax import lax
from jax.experimental import pallas as pl
from jax.experimental.pallas import tpu as pltpu
from jax.sharding import PartitionSpec as P


BLOCK = 128
SEL = 16
QBLK = 128
LAT = 576
LATP = 640
IDXD = 128
IDXH = 64
QPART = 32
ROWS = LAT + IDXD
PAGES = 64

f32 = jnp.float32
bf16 = jnp.bfloat16

LOG2E = math.log2(math.e)
softmax_scale = 192.0 ** (-0.5)
loss_scale = 2048.0


def dot(a, b):
    return lax.dot_general(a, b, (((1,), (0,)), ((), ())), preferred_element_type=f32)


def dot_nt(a, b):
    return lax.dot_general(a, b, (((1,), (1,)), ((), ())), preferred_element_type=f32)


def whole(a):
    return pl.BlockSpec(a.shape, lambda *i: (0,) * a.ndim)


def lookup_body(lists_ref, place_ref, out_ref):
    for k in range(SEL):
        for b in range(2):
            out_ref[k, b] = place_ref[lists_ref[b, k]] & (PAGES - 1)


def lookup(lists, place):
    smem = pl.BlockSpec(memory_space=pltpu.SMEM)
    return pl.pallas_call(
        lookup_body,
        out_shape=jax.ShapeDtypeStruct((SEL, 2), jnp.int32),
        in_specs=[smem, smem],
        out_specs=smem,
        name="lookup",
    )(lists, place)


def pack_body(core_ref, wanted_ref, lat_ref, key_ref, out_ref, sems):
    copies = []
    slots_ref = [wanted_ref[i, core_ref[0]] for i in range(SEL)]
    for i in range(SEL):
        copies.append(pltpu.make_async_copy(lat_ref.at[slots_ref[i]], out_ref.at[i, :LAT, :], sems.at[2 * i]))
        copies.append(pltpu.make_async_copy(key_ref.at[slots_ref[i]], out_ref.at[i, LAT:, :], sems.at[2 * i + 1]))
    for c in copies:
        c.start()
    for c in copies:
        c.wait()


def pack_pages(core, wanted, lat, keys):
    return pl.pallas_call(
        pack_body,
        out_shape=jax.ShapeDtypeStruct((SEL, ROWS, BLOCK), bf16),
        in_specs=[
            pl.BlockSpec(memory_space=pltpu.SMEM),
            pl.BlockSpec(memory_space=pltpu.SMEM),
            pl.BlockSpec(memory_space=pl.ANY),
            pl.BlockSpec(memory_space=pl.ANY),
        ],
        out_specs=pl.BlockSpec(memory_space=pltpu.VMEM),
        scratch_shapes=[pltpu.SemaphoreType.DMA((2 * SEL,))],
        cost_estimate=pl.CostEstimate(flops=0, bytes_accessed=6 << 20, transcendentals=0),
        name="pack_pages",
    )(core, wanted, lat, keys)


def flip_body(place_ref, qo_ref, qs_ref, lo_ref, ls_ref, own_ref, send_ref, lown_ref, lsend_ref):
    to = [pl.ds(pl.multiple_of(((k + 3 - place_ref[1]) & 3) * QPART, QPART), QPART) for k in range(4)]
    for q_ref, o_ref in ((qo_ref, own_ref), (qs_ref, send_ref)):
        for h in range(q_ref.shape[0]):
            rows = q_ref[h].T
            for k in range(4):
                o_ref[h, to[k], :LAT] = rows[k * QPART : (k + 1) * QPART]
            o_ref[h, :, LAT:] = jnp.zeros((QBLK, LATP - LAT), bf16)

    @pl.when(pl.program_id(0) == 0)
    def _():
        for l_ref, o_ref in ((lo_ref, lown_ref), (ls_ref, lsend_ref)):
            o_ref[...] = jnp.zeros_like(o_ref)
            rows = l_ref[...].T * LOG2E
            for k in range(4):
                o_ref[to[k], : l_ref.shape[0]] = rows[k * QPART : (k + 1) * QPART]


def flip_queries(place, qt, lt):
    heads = qt.shape[0]
    hb = 4
    qspec = lambda own: pl.BlockSpec((hb, LAT, QBLK), lambda i, c: (i, 0, c[0] if own else 1 - c[0]))
    lspec = lambda own: pl.BlockSpec((heads, QBLK), lambda i, c: (0, c[0] if own else 1 - c[0]))
    oq = jax.ShapeDtypeStruct((heads, QBLK, LATP), bf16)
    ol = jax.ShapeDtypeStruct((QBLK, 128), f32)
    oqs = pl.BlockSpec((hb, QBLK, LATP), lambda i, c: (i, 0, 0))
    ols = pl.BlockSpec((QBLK, 128), lambda i, c: (0, 0))
    return pl.pallas_call(
        flip_body,
        out_shape=(oq, oq, ol, ol),
        grid_spec=pltpu.PrefetchScalarGridSpec(
            num_scalar_prefetch=1,
            grid=(heads // hb,),
            in_specs=[qspec(True), qspec(False), lspec(True), lspec(False)],
            out_specs=(oqs, oqs, ols, ols),
        ),
        cost_estimate=pl.CostEstimate(flops=0, bytes_accessed=24 << 20, transcendentals=0),
        name="flip_queries",
    )(place, qt, qt, lt, lt)


def first_query(h):
    return pl.multiple_of((h & 1) * QBLK + (h >> 1) * QPART, QPART)


def deal_body(head_ref, iq_ref, w_ref, *refs):
    *out_refs, wt_ref = refs
    wt_ref[...] = w_ref[...].T
    for k in range(8):
        q0 = first_query((head_ref[0] + k) & 7)
        rows = pltpu.einshape("qed->eqd", iq_ref[pl.ds(q0, QPART)].astype(f32))
        out_refs[k][: 8 * QPART, :] = rows.reshape(8 * QPART, IDXD).astype(bf16)
        rest = wt_ref[pl.ds(q0, QPART), :]
        pieces = []
        for _ in range(3):
            piece = rest.astype(bf16).astype(f32)
            pieces.append(piece)
            rest = rest - piece
        pieces.append(jnp.zeros((QPART, IDXD - 24), f32))
        out_refs[k][8 * QPART :, :] = jnp.concatenate(pieces, axis=1).astype(bf16)


def deal(head, iq, wt):
    vmem = pl.BlockSpec(memory_space=pltpu.VMEM)
    return pl.pallas_call(
        deal_body,
        out_shape=[jax.ShapeDtypeStruct((9 * QPART, IDXD), bf16)] * 8,
        in_specs=[pl.BlockSpec(memory_space=pltpu.SMEM), vmem, vmem],
        out_specs=[vmem] * 8,
        scratch_shapes=[pltpu.VMEM((2 * QBLK, 8), f32)],
        cost_estimate=pl.CostEstimate(flops=0, bytes_accessed=2 << 20, transcendentals=0),
        name="deal",
    )(head, iq, wt)


def place_body(head_ref, *refs):
    *in_refs, gq_ref, gw_ref, wt_ref = refs
    for k in range(8):
        q0 = first_query((head_ref[0] + k) & 7)
        rows = in_refs[k][: 8 * QPART, :].astype(f32).reshape(8, QPART, IDXD)
        gq_ref[pl.ds(q0, QPART)] = pltpu.einshape("eqd->qed", rows)
        w = in_refs[k][8 * QPART :, :].astype(f32)
        wt_ref[pl.ds(q0, QPART), :] = w[:, :8] + w[:, 8:16] + w[:, 16:24]
    gw_ref[...] = wt_ref[...].T


def place(head, blocks):
    vmem = pl.BlockSpec(memory_space=pltpu.VMEM)
    return pl.pallas_call(
        place_body,
        out_shape=(jax.ShapeDtypeStruct((2 * QBLK, 8, IDXD), f32), jax.ShapeDtypeStruct((8, 2 * QBLK), f32)),
        in_specs=[pl.BlockSpec(memory_space=pltpu.SMEM)] + [vmem] * 8,
        out_specs=(vmem, vmem),
        scratch_shapes=[pltpu.VMEM((2 * QBLK, 8), f32)],
        cost_estimate=pl.CostEstimate(flops=0, bytes_accessed=2 << 20, transcendentals=0),
        name="place",
    )(head, *blocks)


def add_pages_body(wanted_ref, gk_ref, out_ref):
    out_ref[...] = jnp.zeros_like(out_ref)
    for i in range(SEL):
        for b in range(2):
            rows = [gk_ref[i * 8 + 2 * x + b].astype(f32) for x in range(4)]
            out_ref[wanted_ref[i, b]] += (rows[0] + rows[1]) + (rows[2] + rows[3])


def add_pages(wanted, gk):
    vmem = pl.BlockSpec(memory_space=pltpu.VMEM)
    return pl.pallas_call(
        add_pages_body,
        out_shape=jax.ShapeDtypeStruct((PAGES, 16, IDXD), f32),
        in_specs=[pl.BlockSpec(memory_space=pltpu.SMEM), vmem],
        out_specs=vmem,
        cost_estimate=pl.CostEstimate(flops=0, bytes_accessed=1 << 20, transcendentals=0),
        name="add_pages",
    )(wanted, gk)


HG = 8
PT = 4


def teacher_body(qa_ref, qb_ref, la_ref, lb_ref, kj_ref, t1_ref, t2_ref, t3_ref, own_ref):
    keys = jnp.concatenate([kj_ref[p, :LATP, :] for p in range(PT)], axis=1)
    acc = None
    for q_ref, l_ref in ((qa_ref, la_ref), (qb_ref, lb_ref)):
        for g in range(q_ref.shape[0] // HG):
            s = dot(q_ref[g * HG : (g + 1) * HG].reshape(HG * QBLK, LATP), keys)
            for k in range(HG):
                h = g * HG + k
                part = jnp.exp2(s[k * QBLK : (k + 1) * QBLK] * (softmax_scale * LOG2E) - l_ref[:, h : h + 1])
                acc = part if acc is None else acc + part
    for k, ref in enumerate((t1_ref, t2_ref, t3_ref, own_ref)):
        ref[...] = acc[k * QPART : (k + 1) * QPART].astype(ref.dtype)


def teacher_terms(qa, qb, la, lb, kj):
    n = kj.shape[0]
    spec = pl.BlockSpec((QPART, PT * BLOCK), lambda i: (0, i))
    return pl.pallas_call(
        teacher_body,
        out_shape=[jax.ShapeDtypeStruct((QPART, n * BLOCK), t) for t in (bf16, bf16, bf16, f32)],
        grid=(n // PT,),
        in_specs=[whole(qa), whole(qb), whole(la), whole(lb), pl.BlockSpec((PT, ROWS, BLOCK), lambda i: (i, 0, 0))],
        out_specs=[spec] * 4,
        cost_estimate=pl.CostEstimate(
            flops=2 * 32 * QBLK * n * BLOCK * LAT, bytes_accessed=12 << 20, transcendentals=32 * QBLK * n * BLOCK
        ),
        name="teacher_terms",
    )(qa, qb, la, lb, kj)


PS = 4


def score_body(iq_ref, kj_ref, out_ref, wb_ref):
    @pl.when(pl.program_id(0) == 0)
    def _():
        for src in range(8):
            rows = iq_ref[src, 8 * QPART :, :].astype(f32)
            for i in range(8):
                col = rows[:, i : i + 1] + rows[:, 8 + i : 9 + i] + rows[:, 16 + i : 17 + i]
                wb_ref[src * 8 + i] = jnp.broadcast_to(col, (QPART, 128))

    keys = kj_ref[:, LAT:, :].reshape(-1, IDXD)
    raw = dot_nt(iq_ref[:, : 8 * QPART, :].reshape(IDXH * QPART, IDXD), keys)
    for t in range(PS):
        acc = None
        for e in range(IDXH):
            r = raw[e * QPART : (e + 1) * QPART, t * 128 : (t + 1) * 128]
            part = jnp.maximum(r, 0.0) * wb_ref[e]
            acc = part if acc is None else acc + part
        out_ref[:, t * 128 : (t + 1) * 128] = acc


def scores(iq, kj):
    n = kj.shape[0]
    return pl.pallas_call(
        score_body,
        out_shape=(
            jax.ShapeDtypeStruct((QPART, n * BLOCK), f32),
            jax.ShapeDtypeStruct((IDXH, QPART, 128), f32),
        ),
        grid=(n // PS,),
        in_specs=[whole(iq), pl.BlockSpec((PS, ROWS, BLOCK), lambda i: (i, 0, 0))],
        out_specs=(
            pl.BlockSpec((QPART, PS * BLOCK), lambda i: (0, i)),
            pl.BlockSpec((IDXH, QPART, 128), lambda i: (0, 0, 0)),
        ),
        cost_estimate=pl.CostEstimate(flops=2 * IDXH * QPART * n * BLOCK * IDXD, bytes_accessed=6 << 20, transcendentals=0),
        name="scores",
    )(iq, kj)


PB = 4


def backward_body(own_ref, t1_ref, t2_ref, t3_ref, score_ref, iq_ref, iqt_ref, wb_ref, kj_ref, gk_ref, *refs):
    *gq_refs, grad_ref, gr_ref, gw_ref, acc_ref = refs
    step = pl.program_id(0)
    span = PB * BLOCK

    @pl.when(step == 0)
    def _():
        teacher = own_ref[...] + t1_ref[...].astype(f32) + t2_ref[...].astype(f32) + t3_ref[...].astype(f32)
        target = teacher / jnp.sum(teacher, axis=1, keepdims=True)
        score = score_ref[...]
        e = jnp.exp(score - jnp.max(score, axis=1, keepdims=True))
        probs = e / jnp.sum(e, axis=1, keepdims=True)
        grad_ref[...] = loss_scale * (probs - target)
        acc_ref[...] = jnp.zeros_like(acc_ref)
        gw_ref[...] = jnp.zeros_like(gw_ref)

    keys = kj_ref[:, LAT:, :].reshape(-1, IDXD)
    raw = dot_nt(iq_ref[:, : 8 * QPART, :].reshape(IDXH * QPART, IDXD), keys)
    for e in range(IDXH):
        gsum = gw_ref[e]
        w = wb_ref[e]
        for t in range(PB):
            g = grad_ref[:, pl.ds(pl.multiple_of(step * span + t * 128, 128), 128)]
            r = raw[e * QPART : (e + 1) * QPART, t * 128 : (t + 1) * 128]
            gsum = gsum + g * jnp.maximum(r, 0.0)
            gr_ref[e * QPART : (e + 1) * QPART, t * 128 : (t + 1) * 128] = jnp.where(r > 0.0, g * w, 0.0).astype(bf16)
        gw_ref[e] = gsum
    gr = gr_ref[...]
    gk_ref[...] = dot(iqt_ref[...], gr).T.astype(gk_ref.dtype)
    acc_ref[...] += dot(gr, keys)

    @pl.when(step == pl.num_programs(0) - 1)
    def _():
        lane = lax.broadcasted_iota(jnp.int32, (QPART, 128), 1)
        for src in range(8):
            gq_refs[src][: 8 * QPART, :] = acc_ref[src * 8 * QPART : (src + 1) * 8 * QPART, :].astype(bf16)
            out = jnp.zeros((QPART, 128), f32)
            for i in range(8):
                rest = jnp.sum(gw_ref[src * 8 + i], axis=1, keepdims=True)
                for k in range(3):
                    piece = rest.astype(bf16).astype(f32)
                    out = jnp.where(lane == 8 * k + i, piece, out)
                    rest = rest - piece
            gq_refs[src][8 * QPART :, :] = out.astype(bf16)


def backward(own, moved, score, iq, iqt, wb, kj):
    n = kj.shape[0]
    fixed = (own, *moved, score, iq, iqt, wb)
    return pl.pallas_call(
        backward_body,
        out_shape=(
            jax.ShapeDtypeStruct((n * BLOCK, IDXD), bf16),
        )
        + (jax.ShapeDtypeStruct((9 * QPART, IDXD), bf16),) * 8,
        grid=(n // PB,),
        in_specs=[whole(a) for a in fixed] + [pl.BlockSpec((PB, ROWS, BLOCK), lambda i: (i, 0, 0))],
        out_specs=(
            pl.BlockSpec((PB * BLOCK, IDXD), lambda i: (i, 0)),
        )
        + (pl.BlockSpec((9 * QPART, IDXD), lambda i: (0, 0)),) * 8,
        scratch_shapes=[
            pltpu.VMEM((QPART, n * BLOCK), f32),
            pltpu.VMEM((IDXH * QPART, PB * BLOCK), bf16),
            pltpu.VMEM((IDXH, QPART, 128), f32),
            pltpu.VMEM((IDXH * QPART, IDXD), f32),
        ],
        cost_estimate=pl.CostEstimate(flops=6 * IDXH * QPART * n * BLOCK * IDXD, bytes_accessed=8 << 20, transcendentals=0),
        name="backward",
    )(*fixed, kj)


def step(queries, lse, latent, index_keys, index_queries, index_weights, block_lists, block_place):
    head = lax.axis_index("head")
    core = head & 1
    quarter = head >> 1
    partner = [(h, h ^ 1) for h in range(8)]

    wanted = lookup(block_lists, block_place).reshape(SEL, 1, 2)
    wanted = lax.all_to_all(wanted, "seq", split_axis=0, concat_axis=0, tiled=True).reshape(SEL, 2)

    packed = pack_pages(core.reshape(1), wanted, latent.transpose(0, 2, 1), index_keys)
    kj = lax.all_to_all(packed, "seq", split_axis=0, concat_axis=0, tiled=True)

    dealt = [*deal(head.reshape(1), index_queries, index_weights.T)]
    dealt = dealt[:1] + [lax.ppermute(dealt[k], "head", [(h, (h + k) & 7) for h in range(8)]) for k in range(1, 8)]
    iq = jnp.stack(dealt)
    iqt = iq[:, : 8 * QPART].reshape(IDXH * QPART, IDXD).T

    qa, qs, la, ls = flip_queries(jnp.stack([core, quarter]), queries.transpose(1, 2, 0), lse.T)
    qb = lax.ppermute(qs, "head", partner)
    lb = lax.ppermute(ls, "head", partner)

    *parts, own = teacher_terms(qa, qb, la, lb, kj)
    moved = []
    for d in (2, 1, 3):
        ring = [(2 * x + c, 2 * ((x + d) % 4) + c) for x in range(4) for c in range(2)]
        moved.append(lax.ppermute(parts[d - 1], "head", ring))
    score, wb = scores(iq, kj)

    gk, *gq = backward(own, moved, score, iq, iqt, wb, kj)

    gk = lax.all_to_all(gk.reshape(128, 16, IDXD), ("seq", "head"), split_axis=0, concat_axis=0, tiled=True)
    gq = gq[:1] + [lax.ppermute(gq[k], "head", [(h, (h - k) & 7) for h in range(8)]) for k in range(1, 8)]
    gq, gw = place(head.reshape(1), gq)
    return gq, gw.T, add_pages(wanted, gk)


def solution(mesh):
    return jax.shard_map(
        step,
        mesh=mesh,
        in_specs=(
            P("seq", "head", None),
            P("seq", "head"),
            P("seq", None, None),
            P("seq", None, None),
            P("seq", "head", None),
            P("seq", "head"),
            P("seq", None),
            P(),
        ),
        out_specs=(P("seq", "head", None), P("seq", "head"), P("seq", "head", None)),
        check_vma=False,
    )
```

```python
import math

import jax
import jax.numpy as jnp
from jax import lax
from jax.experimental import pallas as pl
from jax.experimental.pallas import tpu as pltpu
from jax.sharding import PartitionSpec as P


BLOCK = 128
SEL = 16
QBLK = 128
LAT = 576
LATP = 640
IDXD = 128
IDXH = 64
QPART = 32
ROWS = LAT + IDXD
PAGES = 64

f32 = jnp.float32
bf16 = jnp.bfloat16

LOG2E = math.log2(math.e)
softmax_scale = 192.0 ** (-0.5)
loss_scale = 2048.0


def dot(a, b):
    return lax.dot_general(a, b, (((1,), (0,)), ((), ())), preferred_element_type=f32)


def dot_nt(a, b):
    return lax.dot_general(a, b, (((1,), (1,)), ((), ())), preferred_element_type=f32)


def whole(a):
    return pl.BlockSpec(a.shape, lambda *i: (0,) * a.ndim)


def lookup_body(lists_ref, place_ref, out_ref):
    for k in range(SEL):
        for b in range(2):
            out_ref[k, b] = place_ref[lists_ref[b, k]] & (PAGES - 1)


def lookup(lists, place):
    smem = pl.BlockSpec(memory_space=pltpu.SMEM)
    return pl.pallas_call(
        lookup_body,
        out_shape=jax.ShapeDtypeStruct((SEL, 2), jnp.int32),
        in_specs=[smem, smem],
        out_specs=smem,
        name="lookup",
    )(lists, place)


def pack_body(core_ref, wanted_ref, lat_ref, key_ref, out_ref, pages, sems, done):
    reads, writes = [], []
    for i in range(SEL):
        slot = wanted_ref[i, core_ref[0]]
        reads.append(
            (
                pltpu.make_async_copy(lat_ref.at[slot], pages.at[i, pl.ds(BLOCK, LAT), :], sems.at[2 * i]),
                pltpu.make_async_copy(key_ref.at[slot], pages.at[i, pl.ds(0, BLOCK), :], sems.at[2 * i + 1]),
            )
        )
        writes.append(pltpu.make_async_copy(pages.at[i], out_ref.at[i], done.at[i]))
    for pair in reads:
        for c in pair:
            c.start()
    for pair, w in zip(reads, writes):
        for c in pair:
            c.wait()
        w.start()
    for w in writes:
        w.wait()


def pack_pages(core, wanted, lat, keys):
    return pl.pallas_call(
        pack_body,
        out_shape=jax.ShapeDtypeStruct((SEL, ROWS, BLOCK), bf16),
        in_specs=[
            pl.BlockSpec(memory_space=pltpu.SMEM),
            pl.BlockSpec(memory_space=pltpu.SMEM),
            pl.BlockSpec(memory_space=pl.ANY),
            pl.BlockSpec(memory_space=pl.ANY),
        ],
        out_specs=pl.BlockSpec(memory_space=pl.ANY),
        scratch_shapes=[
            pltpu.VMEM((SEL, ROWS, BLOCK), bf16),
            pltpu.SemaphoreType.DMA((2 * SEL,)),
            pltpu.SemaphoreType.DMA((SEL,)),
        ],
        cost_estimate=pl.CostEstimate(flops=0, bytes_accessed=6 << 20, transcendentals=0),
        name="pack_pages",
    )(core, wanted, lat, keys)


def flip_body(place_ref, qo_ref, qs_ref, lo_ref, ls_ref, own_ref, send_ref, lown_ref, lsend_ref):
    to = [pl.ds(pl.multiple_of(((k + 3 - place_ref[1]) & 3) * QPART, QPART), QPART) for k in range(4)]
    for q_ref, o_ref in ((qo_ref, own_ref), (qs_ref, send_ref)):
        for h in range(q_ref.shape[0]):
            rows = q_ref[h].T
            for k in range(4):
                o_ref[h, to[k], :LAT] = rows[k * QPART : (k + 1) * QPART]
            o_ref[h, :, LAT:] = jnp.zeros((QBLK, LATP - LAT), bf16)

    @pl.when(pl.program_id(0) == 0)
    def _():
        for l_ref, o_ref in ((lo_ref, lown_ref), (ls_ref, lsend_ref)):
            o_ref[...] = jnp.zeros_like(o_ref)
            rows = l_ref[...].T * LOG2E
            for k in range(4):
                o_ref[to[k], : l_ref.shape[0]] = rows[k * QPART : (k + 1) * QPART]


def flip_queries(place, qt, lt):
    heads = qt.shape[0]
    hb = 4
    qspec = lambda own: pl.BlockSpec((hb, LAT, QBLK), lambda i, c: (i, 0, c[0] if own else 1 - c[0]))
    lspec = lambda own: pl.BlockSpec((heads, QBLK), lambda i, c: (0, c[0] if own else 1 - c[0]))
    oq = jax.ShapeDtypeStruct((heads, QBLK, LATP), bf16)
    ol = jax.ShapeDtypeStruct((QBLK, 128), f32)
    oqs = pl.BlockSpec((hb, QBLK, LATP), lambda i, c: (i, 0, 0))
    ols = pl.BlockSpec((QBLK, 128), lambda i, c: (0, 0))
    return pl.pallas_call(
        flip_body,
        out_shape=(oq, oq, ol, ol),
        grid_spec=pltpu.PrefetchScalarGridSpec(
            num_scalar_prefetch=1,
            grid=(heads // hb,),
            in_specs=[qspec(True), qspec(False), lspec(True), lspec(False)],
            out_specs=(oqs, oqs, ols, ols),
        ),
        cost_estimate=pl.CostEstimate(flops=0, bytes_accessed=24 << 20, transcendentals=0),
        name="flip_queries",
    )(place, qt, qt, lt, lt)


def first_query(h):
    return pl.multiple_of((h & 1) * QBLK + (h >> 1) * QPART, QPART)


def deal_body(head_ref, iq_ref, w_ref, *refs):
    *out_refs, wt_ref = refs
    wt_ref[...] = w_ref[...].T
    for k in range(8):
        q0 = first_query((head_ref[0] + k) & 7)
        rows = pltpu.einshape("qed->eqd", iq_ref[pl.ds(q0, QPART)].astype(f32))
        out_refs[k][: 8 * QPART, :] = rows.reshape(8 * QPART, IDXD).astype(bf16)
        rest = wt_ref[pl.ds(q0, QPART), :]
        pieces = []
        for _ in range(3):
            piece = rest.astype(bf16).astype(f32)
            pieces.append(piece)
            rest = rest - piece
        pieces.append(jnp.zeros((QPART, IDXD - 24), f32))
        out_refs[k][8 * QPART :, :] = jnp.concatenate(pieces, axis=1).astype(bf16)


def deal(head, iq, wt):
    vmem = pl.BlockSpec(memory_space=pltpu.VMEM)
    return pl.pallas_call(
        deal_body,
        out_shape=[jax.ShapeDtypeStruct((9 * QPART, IDXD), bf16)] * 8,
        in_specs=[pl.BlockSpec(memory_space=pltpu.SMEM), vmem, vmem],
        out_specs=[vmem] * 8,
        scratch_shapes=[pltpu.VMEM((2 * QBLK, 8), f32)],
        cost_estimate=pl.CostEstimate(flops=0, bytes_accessed=2 << 20, transcendentals=0),
        name="deal",
    )(head, iq, wt)


def place_body(head_ref, *refs):
    *in_refs, gq_ref, gw_ref, wt_ref = refs
    for k in range(8):
        q0 = first_query((head_ref[0] + k) & 7)
        rows = in_refs[k][: 8 * QPART, :].astype(f32).reshape(8, QPART, IDXD)
        gq_ref[pl.ds(q0, QPART)] = pltpu.einshape("eqd->qed", rows)
        w = in_refs[k][8 * QPART :, :].astype(f32)
        wt_ref[pl.ds(q0, QPART), :] = w[:, :8] + w[:, 8:16] + w[:, 16:24]
    gw_ref[...] = wt_ref[...].T


def place(head, blocks):
    vmem = pl.BlockSpec(memory_space=pltpu.VMEM)
    return pl.pallas_call(
        place_body,
        out_shape=(jax.ShapeDtypeStruct((2 * QBLK, 8, IDXD), f32), jax.ShapeDtypeStruct((8, 2 * QBLK), f32)),
        in_specs=[pl.BlockSpec(memory_space=pltpu.SMEM)] + [vmem] * 8,
        out_specs=(vmem, vmem),
        scratch_shapes=[pltpu.VMEM((2 * QBLK, 8), f32)],
        cost_estimate=pl.CostEstimate(flops=0, bytes_accessed=2 << 20, transcendentals=0),
        name="place",
        compiler_params=pltpu.CompilerParams(vmem_limit_bytes=8 << 20),
    )(head, *blocks)


def add_pages_body(wanted_ref, gk_ref, out_ref):
    out_ref[...] = jnp.zeros_like(out_ref)
    for i in range(SEL):
        for b in range(2):
            rows = [gk_ref[i * 8 + 2 * x + b].astype(f32) for x in range(4)]
            out_ref[wanted_ref[i, b]] += (rows[0] + rows[1]) + (rows[2] + rows[3])


def add_pages(wanted, gk):
    vmem = pl.BlockSpec(memory_space=pltpu.VMEM)
    return pl.pallas_call(
        add_pages_body,
        out_shape=jax.ShapeDtypeStruct((PAGES, 16, IDXD), f32),
        in_specs=[pl.BlockSpec(memory_space=pltpu.SMEM), vmem],
        out_specs=vmem,
        cost_estimate=pl.CostEstimate(flops=0, bytes_accessed=1 << 20, transcendentals=0),
        name="add_pages",
        compiler_params=pltpu.CompilerParams(vmem_limit_bytes=4 << 20),
    )(wanted, gk)


HG = 8
PT = 4


def teacher_body(qa_ref, qb_ref, la_ref, lb_ref, kj_ref, t1_ref, t2_ref, t3_ref, own_ref):
    keys = jnp.concatenate([kj_ref[p, BLOCK:, :] for p in range(PT)], axis=1)
    acc = None
    for q_ref, l_ref in ((qa_ref, la_ref), (qb_ref, lb_ref)):
        for g in range(q_ref.shape[0] // HG):
            s = dot(q_ref[g * HG : (g + 1) * HG, :, :LAT].reshape(HG * QBLK, LAT), keys)
            for k in range(HG):
                h = g * HG + k
                part = jnp.exp2(s[k * QBLK : (k + 1) * QBLK] * (softmax_scale * LOG2E) - l_ref[:, h : h + 1])
                acc = part if acc is None else acc + part
    for k, ref in enumerate((t1_ref, t2_ref, t3_ref, own_ref)):
        ref[...] = acc[k * QPART : (k + 1) * QPART].astype(ref.dtype)


def teacher_terms(qa, qb, la, lb, kj):
    n = kj.shape[0]
    spec = pl.BlockSpec((QPART, PT * BLOCK), lambda i: (0, i))
    return pl.pallas_call(
        teacher_body,
        out_shape=[jax.ShapeDtypeStruct((QPART, n * BLOCK), t) for t in (bf16, bf16, bf16, f32)],
        grid=(n // PT,),
        in_specs=[whole(qa), whole(qb), whole(la), whole(lb), pl.BlockSpec((PT, ROWS, BLOCK), lambda i: (i, 0, 0))],
        out_specs=[spec] * 4,
        cost_estimate=pl.CostEstimate(
            flops=2 * 32 * QBLK * n * BLOCK * LAT, bytes_accessed=12 << 20, transcendentals=32 * QBLK * n * BLOCK
        ),
        name="teacher_terms",
        compiler_params=pltpu.CompilerParams(vmem_limit_bytes=24 << 20),
    )(qa, qb, la, lb, kj)


def spread_body(*refs):
    *in_refs, iq_ref, iqt_ref, wb_ref = refs
    for src in range(8):
        rows = in_refs[src][: 8 * QPART, :]
        iq_ref[src * 8 * QPART : (src + 1) * 8 * QPART, :] = rows
        iqt_ref[:, src * 8 * QPART : (src + 1) * 8 * QPART] = rows.T
        w = in_refs[src][8 * QPART :, :].astype(f32)
        for i in range(8):
            col = w[:, i : i + 1] + w[:, 8 + i : 9 + i] + w[:, 16 + i : 17 + i]
            wb_ref[src * 8 + i] = jnp.broadcast_to(col, (QPART, 128))


def spread(blocks):
    vmem = pl.BlockSpec(memory_space=pltpu.VMEM)
    return pl.pallas_call(
        spread_body,
        out_shape=(
            jax.ShapeDtypeStruct((IDXH * QPART, IDXD), bf16),
            jax.ShapeDtypeStruct((IDXD, IDXH * QPART), bf16),
            jax.ShapeDtypeStruct((IDXH, QPART, 128), f32),
        ),
        in_specs=[vmem] * 8,
        out_specs=(vmem,) * 3,
        cost_estimate=pl.CostEstimate(flops=0, bytes_accessed=3 << 20, transcendentals=0),
        name="spread",
    )(*blocks)


PS = 4


def score_body(iq_ref, wb_ref, kj_ref, out_ref, raw_ref):
    raw = dot_nt(iq_ref[...], kj_ref[...].reshape(-1, IDXD))
    raw_ref[...] = raw.astype(bf16)
    for t in range(PS):
        acc = None
        for e in range(IDXH):
            r = raw[e * QPART : (e + 1) * QPART, t * 128 : (t + 1) * 128]
            part = jnp.maximum(r, 0.0) * wb_ref[e]
            acc = part if acc is None else acc + part
        out_ref[:, t * 128 : (t + 1) * 128] = acc


def scores(iq, wb, kj):
    n = kj.shape[0]
    return pl.pallas_call(
        score_body,
        out_shape=(
            jax.ShapeDtypeStruct((QPART, n * BLOCK), f32),
            jax.ShapeDtypeStruct((IDXH * QPART, n * BLOCK), bf16),
        ),
        grid=(n // PS,),
        in_specs=[whole(iq), whole(wb), pl.BlockSpec((PS, BLOCK, IDXD), lambda i: (i, 0, 0))],
        out_specs=(
            pl.BlockSpec((QPART, PS * BLOCK), lambda i: (0, i)),
            pl.BlockSpec((IDXH * QPART, PS * BLOCK), lambda i: (0, i)),
        ),
        cost_estimate=pl.CostEstimate(flops=2 * IDXH * QPART * n * BLOCK * IDXD, bytes_accessed=12 << 20, transcendentals=0),
        name="scores",
    )(iq, wb, kj)


PB = 4


def backward_body(own_ref, t1_ref, t2_ref, t3_ref, score_ref, iq_ref, iqt_ref, wb_ref, raw_ref, kj_ref, gk_ref, *refs):
    *gq_refs, grad_ref, gr_ref, acc_ref = refs
    step = pl.program_id(0)
    span = PB * BLOCK

    @pl.when(step == 0)
    def _():
        teacher = own_ref[...] + t1_ref[...].astype(f32) + t2_ref[...].astype(f32) + t3_ref[...].astype(f32)
        target = teacher / jnp.sum(teacher, axis=1, keepdims=True)
        score = score_ref[...]
        e = jnp.exp(score - jnp.max(score, axis=1, keepdims=True))
        probs = e / jnp.sum(e, axis=1, keepdims=True)
        grad_ref[...] = loss_scale * (probs - target)
        acc_ref[...] = jnp.zeros_like(acc_ref)

    keys = kj_ref[...].reshape(-1, IDXD)
    for t in range(PB):
        g = grad_ref[:, pl.ds(pl.multiple_of(step * span + t * 128, 128), 128)]
        at = slice(t * 128, (t + 1) * 128)
        for e in range(IDXH):
            rows = slice(e * QPART, (e + 1) * QPART)
            gr_ref[rows, at] = jnp.where(raw_ref[rows, at] > 0, (g * wb_ref[e]).astype(bf16), 0)
    gr = gr_ref[...]
    gk_ref[...] = dot(iqt_ref[...], gr).T.astype(gk_ref.dtype)
    acc_ref[...] += dot(gr, keys)

    @pl.when(step == pl.num_programs(0) - 1)
    def _():
        lane = lax.broadcasted_iota(jnp.int32, (QPART, 128), 1)
        for src in range(8):
            gq_refs[src][: 8 * QPART, :] = acc_ref[src * 8 * QPART : (src + 1) * 8 * QPART, :].astype(bf16)
            out = jnp.zeros((QPART, 128), f32)
            for i in range(8):
                e = src * 8 + i
                rows = slice(e * QPART, (e + 1) * QPART)
                gw = jnp.sum(iq_ref[rows, :].astype(f32) * acc_ref[rows, :], axis=1, keepdims=True)
                rest = gw / wb_ref[e]
                for k in range(3):
                    piece = rest.astype(bf16).astype(f32)
                    out = jnp.where(lane == 8 * k + i, piece, out)
                    rest = rest - piece
            gq_refs[src][8 * QPART :, :] = out.astype(bf16)


def backward(own, moved, score, iq, iqt, wb, raw, kj):
    n = kj.shape[0]
    fixed = (own, *moved, score, iq, iqt, wb)
    return pl.pallas_call(
        backward_body,
        out_shape=(jax.ShapeDtypeStruct((n * BLOCK, IDXD), bf16),)
        + (jax.ShapeDtypeStruct((9 * QPART, IDXD), bf16),) * 8,
        grid=(n // PB,),
        in_specs=[whole(a) for a in fixed]
        + [
            pl.BlockSpec((IDXH * QPART, PB * BLOCK), lambda i: (0, i)),
            pl.BlockSpec((PB, BLOCK, IDXD), lambda i: (i, 0, 0)),
        ],
        out_specs=(pl.BlockSpec((PB * BLOCK, IDXD), lambda i: (i, 0)),)
        + (pl.BlockSpec((9 * QPART, IDXD), lambda i: (0, 0)),) * 8,
        scratch_shapes=[
            pltpu.VMEM((QPART, n * BLOCK), f32),
            pltpu.VMEM((IDXH * QPART, PB * BLOCK), bf16),
            pltpu.VMEM((IDXH * QPART, IDXD), f32),
        ],
        cost_estimate=pl.CostEstimate(flops=4 * IDXH * QPART * n * BLOCK * IDXD, bytes_accessed=16 << 20, transcendentals=0),
        name="backward",
    )(*fixed, raw, kj)


def step(queries, lse, latent, index_keys, index_queries, index_weights, block_lists, block_place):
    head = lax.axis_index("head")
    core = head & 1
    quarter = head >> 1
    partner = [(h, h ^ 1) for h in range(8)]

    wanted = lookup(block_lists, block_place).reshape(SEL, 1, 2)
    wanted = lax.all_to_all(wanted, "seq", split_axis=0, concat_axis=0, tiled=True).reshape(SEL, 2)

    packed = pack_pages(core.reshape(1), wanted, latent.transpose(0, 2, 1), index_keys)
    kj = lax.all_to_all(packed, "seq", split_axis=0, concat_axis=0, tiled=True)

    dealt = [*deal(head.reshape(1), index_queries, index_weights.T)]
    dealt = dealt[:1] + [lax.ppermute(dealt[k], "head", [(h, (h + k) & 7) for h in range(8)]) for k in range(1, 8)]
    iq, iqt, wb = spread(dealt)

    qa, qs, la, ls = flip_queries(jnp.stack([core, quarter]), queries.transpose(1, 2, 0), lse.T)
    qb = lax.ppermute(qs, "head", partner)
    lb = lax.ppermute(ls, "head", partner)

    *parts, own = teacher_terms(qa, qb, la, lb, kj)
    moved = []
    for d in (2, 1, 3):
        ring = [(2 * x + c, 2 * ((x + d) % 4) + c) for x in range(4) for c in range(2)]
        moved.append(lax.ppermute(parts[d - 1], "head", ring))
    score, raw = scores(iq, wb, kj)

    gk, *gq = backward(own, moved, score, iq, iqt, wb, raw, kj)

    gk = lax.all_to_all(gk.reshape(128, 16, IDXD), ("seq", "head"), split_axis=0, concat_axis=0, tiled=True)
    gq = gq[:1] + [lax.ppermute(gq[k], "head", [(h, (h - k) & 7) for h in range(8)]) for k in range(1, 8)]
    gq, gw = place(head.reshape(1), gq)
    return gq, gw.T, add_pages(wanted, gk)


def solution(mesh):
    return jax.shard_map(
        step,
        mesh=mesh,
        in_specs=(
            P("seq", "head", None),
            P("seq", "head"),
            P("seq", None, None),
            P("seq", None, None),
            P("seq", "head", None),
            P("seq", "head"),
            P("seq", None),
            P(),
        ),
        out_specs=(P("seq", "head", None), P("seq", "head"), P("seq", "head", None)),
        check_vma=False,
    )
```

```python
import math

import jax
import jax.numpy as jnp
from jax import lax
from jax.experimental import pallas as pl
from jax.experimental.pallas import tpu as pltpu
from jax.sharding import PartitionSpec as P


BLOCK = 128
SEL = 16
QBLK = 128
LAT = 576
LATP = 640
IDXD = 128
IDXH = 64
QPART = 32
ROWS = LAT + IDXD
PAGES = 64

f32 = jnp.float32
bf16 = jnp.bfloat16

LOG2E = math.log2(math.e)
softmax_scale = 192.0 ** (-0.5)
loss_scale = 2048.0


def dot(a, b):
    return lax.dot_general(a, b, (((1,), (0,)), ((), ())), preferred_element_type=f32)


def dot_nt(a, b):
    return lax.dot_general(a, b, (((1,), (1,)), ((), ())), preferred_element_type=f32)


def whole(a):
    return pl.BlockSpec(a.shape, lambda *i: (0,) * a.ndim)


def lookup_body(lists_ref, place_ref, out_ref):
    for k in range(SEL):
        for b in range(2):
            out_ref[k, b] = place_ref[lists_ref[b, k]] & (PAGES - 1)


def lookup(lists, place):
    smem = pl.BlockSpec(memory_space=pltpu.SMEM)
    return pl.pallas_call(
        lookup_body,
        out_shape=jax.ShapeDtypeStruct((SEL, 2), jnp.int32),
        in_specs=[smem, smem],
        out_specs=smem,
        name="lookup",
    )(lists, place)


def pack_body(core_ref, wanted_ref, lat_ref, key_ref, out_ref, pages, sems, done):
    reads, writes = [], []
    for i in range(SEL):
        slot = wanted_ref[i, core_ref[0]]
        reads.append(
            (
                pltpu.make_async_copy(lat_ref.at[slot], pages.at[i, pl.ds(BLOCK, LAT), :], sems.at[2 * i]),
                pltpu.make_async_copy(key_ref.at[slot], pages.at[i, pl.ds(0, BLOCK), :], sems.at[2 * i + 1]),
            )
        )
        writes.append(pltpu.make_async_copy(pages.at[i], out_ref.at[i], done.at[i]))
    for pair in reads:
        for c in pair:
            c.start()
    for pair, w in zip(reads, writes):
        for c in pair:
            c.wait()
        w.start()
    for w in writes:
        w.wait()


def pack_pages(core, wanted, lat, keys):
    return pl.pallas_call(
        pack_body,
        out_shape=jax.ShapeDtypeStruct((SEL, ROWS, BLOCK), bf16),
        in_specs=[
            pl.BlockSpec(memory_space=pltpu.SMEM),
            pl.BlockSpec(memory_space=pltpu.SMEM),
            pl.BlockSpec(memory_space=pl.ANY),
            pl.BlockSpec(memory_space=pl.ANY),
        ],
        out_specs=pl.BlockSpec(memory_space=pl.ANY),
        scratch_shapes=[
            pltpu.VMEM((SEL, ROWS, BLOCK), bf16),
            pltpu.SemaphoreType.DMA((2 * SEL,)),
            pltpu.SemaphoreType.DMA((SEL,)),
        ],
        cost_estimate=pl.CostEstimate(flops=0, bytes_accessed=6 << 20, transcendentals=0),
        name="pack_pages",
    )(core, wanted, lat, keys)


def flip_body(place_ref, qo_ref, qs_ref, lo_ref, ls_ref, own_ref, send_ref, lown_ref, lsend_ref):
    to = [pl.ds(pl.multiple_of(((k + 3 - place_ref[1]) & 3) * QPART, QPART), QPART) for k in range(4)]
    for q_ref, o_ref in ((qo_ref, own_ref), (qs_ref, send_ref)):
        for h in range(q_ref.shape[0]):
            rows = q_ref[h].T
            for k in range(4):
                o_ref[h, to[k], :LAT] = rows[k * QPART : (k + 1) * QPART]
            o_ref[h, :, LAT:] = jnp.zeros((QBLK, LATP - LAT), bf16)

    @pl.when(pl.program_id(0) == 0)
    def _():
        for l_ref, o_ref in ((lo_ref, lown_ref), (ls_ref, lsend_ref)):
            o_ref[...] = jnp.zeros_like(o_ref)
            rows = l_ref[...].T * LOG2E
            for k in range(4):
                o_ref[to[k], : l_ref.shape[0]] = rows[k * QPART : (k + 1) * QPART]


def flip_queries(place, qt, lt):
    heads = qt.shape[0]
    hb = 4
    qspec = lambda own: pl.BlockSpec((hb, LAT, QBLK), lambda i, c: (i, 0, c[0] if own else 1 - c[0]))
    lspec = lambda own: pl.BlockSpec((heads, QBLK), lambda i, c: (0, c[0] if own else 1 - c[0]))
    oq = jax.ShapeDtypeStruct((heads, QBLK, LATP), bf16)
    ol = jax.ShapeDtypeStruct((QBLK, 128), f32)
    oqs = pl.BlockSpec((hb, QBLK, LATP), lambda i, c: (i, 0, 0))
    ols = pl.BlockSpec((QBLK, 128), lambda i, c: (0, 0))
    return pl.pallas_call(
        flip_body,
        out_shape=(oq, oq, ol, ol),
        grid_spec=pltpu.PrefetchScalarGridSpec(
            num_scalar_prefetch=1,
            grid=(heads // hb,),
            in_specs=[qspec(True), qspec(False), lspec(True), lspec(False)],
            out_specs=(oqs, oqs, ols, ols),
        ),
        cost_estimate=pl.CostEstimate(flops=0, bytes_accessed=24 << 20, transcendentals=0),
        name="flip_queries",
    )(place, qt, qt, lt, lt)


def first_query(h):
    return pl.multiple_of((h & 1) * QBLK + (h >> 1) * QPART, QPART)


def deal_body(head_ref, iq_ref, w_ref, *refs):
    *out_refs, wt_ref = refs
    wt_ref[...] = w_ref[...].T
    for k in range(8):
        q0 = first_query((head_ref[0] + k) & 7)
        rows = pltpu.einshape("qed->eqd", iq_ref[pl.ds(q0, QPART)].astype(f32))
        out_refs[k][: 8 * QPART, :] = rows.reshape(8 * QPART, IDXD).astype(bf16)
        rest = wt_ref[pl.ds(q0, QPART), :]
        pieces = []
        for _ in range(3):
            piece = rest.astype(bf16).astype(f32)
            pieces.append(piece)
            rest = rest - piece
        pieces.append(jnp.zeros((QPART, IDXD - 24), f32))
        out_refs[k][8 * QPART :, :] = jnp.concatenate(pieces, axis=1).astype(bf16)


def deal(head, iq, wt):
    vmem = pl.BlockSpec(memory_space=pltpu.VMEM)
    return pl.pallas_call(
        deal_body,
        out_shape=[jax.ShapeDtypeStruct((9 * QPART, IDXD), bf16)] + [pltpu.HBM((9 * QPART, IDXD), bf16)] * 7,
        in_specs=[pl.BlockSpec(memory_space=pltpu.SMEM), vmem, vmem],
        out_specs=[vmem] * 8,
        scratch_shapes=[pltpu.VMEM((2 * QBLK, 8), f32)],
        cost_estimate=pl.CostEstimate(flops=0, bytes_accessed=2 << 20, transcendentals=0),
        name="deal",
        compiler_params=pltpu.CompilerParams(vmem_limit_bytes=4 << 20),
    )(head, iq, wt)


def place_body(head_ref, iq_ref, w_ref, *refs):
    *in_refs, gq_ref, gw_ref, wt_ref = refs
    for k in range(8):
        q0 = first_query((head_ref[0] + k) & 7)
        rows = pltpu.einshape("eqd->qed", in_refs[k][...].astype(f32).reshape(8, QPART, IDXD))
        gq_ref[pl.ds(q0, QPART)] = rows
        wt_ref[pl.ds(q0, QPART), :] = jnp.sum(rows * iq_ref[pl.ds(q0, QPART)].astype(f32), axis=2)
    gw_ref[...] = wt_ref[...].T / w_ref[...]


def place(head, iq, wt, blocks):
    vmem = pl.BlockSpec(memory_space=pltpu.VMEM)
    return pl.pallas_call(
        place_body,
        out_shape=(jax.ShapeDtypeStruct((2 * QBLK, 8, IDXD), f32), jax.ShapeDtypeStruct((8, 2 * QBLK), f32)),
        in_specs=[pl.BlockSpec(memory_space=pltpu.SMEM)] + [vmem] * 10,
        out_specs=(vmem, vmem),
        scratch_shapes=[pltpu.VMEM((2 * QBLK, 8), f32)],
        cost_estimate=pl.CostEstimate(flops=0, bytes_accessed=2 << 20, transcendentals=0),
        name="place",
        compiler_params=pltpu.CompilerParams(vmem_limit_bytes=8 << 20),
    )(head, iq, wt, *blocks)


def add_pages_body(wanted_ref, gk_ref, out_ref):
    out_ref[...] = jnp.zeros_like(out_ref)
    for i in range(SEL):
        for b in range(2):
            rows = [gk_ref[i * 8 + 2 * x + b].astype(f32) for x in range(4)]
            out_ref[wanted_ref[i, b]] += (rows[0] + rows[1]) + (rows[2] + rows[3])


def add_pages(wanted, gk):
    vmem = pl.BlockSpec(memory_space=pltpu.VMEM)
    return pl.pallas_call(
        add_pages_body,
        out_shape=jax.ShapeDtypeStruct((PAGES, 16, IDXD), f32),
        in_specs=[pl.BlockSpec(memory_space=pltpu.SMEM), vmem],
        out_specs=vmem,
        cost_estimate=pl.CostEstimate(flops=0, bytes_accessed=1 << 20, transcendentals=0),
        name="add_pages",
        compiler_params=pltpu.CompilerParams(vmem_limit_bytes=4 << 20),
    )(wanted, gk)


HG = 8
PT = 8


def teacher_body(qa_ref, qb_ref, la_ref, lb_ref, kj_ref, t1_ref, t2_ref, t3_ref, own_ref, q_ref, l_ref, sems):
    half = qa_ref.shape[0]
    copies = []
    lses = [pltpu.make_async_copy(src, l_ref.at[k], sems.at[4 + k]) for k, src in enumerate((la_ref, lb_ref))]
    for c in lses:
        c.start()
    for g in range(2 * half // HG):
        src = (qa_ref, qb_ref)[g * HG // half].at[pl.ds(g * HG % half, HG)]
        copies.append(pltpu.make_async_copy(src, q_ref.at[pl.ds(g * HG, HG)], sems.at[g]))
    for c in copies:
        c.start()
    for c in lses:
        c.wait()
    for i in range(SEL // PT):
        keys = jnp.concatenate([kj_ref[i * PT + p, BLOCK:, :] for p in range(PT)], axis=1)
        acc = None
        for g, c in enumerate(copies):
            if i == 0:
                c.wait()
            s = dot(q_ref[g * HG : (g + 1) * HG, :, :LAT].reshape(HG * QBLK, LAT), keys)
            for k in range(HG):
                side, h = g * HG // half, g * HG % half + k
                part = jnp.exp2(s[k * QBLK : (k + 1) * QBLK] * (softmax_scale * LOG2E) - l_ref[side, :, h : h + 1])
                acc = part if acc is None else acc + part
        at = slice(i * PT * BLOCK, (i + 1) * PT * BLOCK)
        for k, ref in enumerate((t1_ref, t2_ref, t3_ref, own_ref)):
            ref[:, at] = acc[k * QPART : (k + 1) * QPART].astype(ref.dtype)


def teacher_terms(qa, qb, la, lb, kj):
    n = kj.shape[0]
    vmem = pl.BlockSpec(memory_space=pltpu.VMEM)
    hbm = pl.BlockSpec(memory_space=pltpu.HBM)
    heads = 2 * qa.shape[0]
    return pl.pallas_call(
        teacher_body,
        out_shape=[jax.ShapeDtypeStruct((QPART, n * BLOCK), t) for t in (bf16, bf16, bf16, f32)],
        in_specs=[hbm, hbm, hbm, hbm, vmem],
        out_specs=[vmem] * 4,
        scratch_shapes=[
            pltpu.VMEM((heads, QBLK, LATP), bf16),
            pltpu.VMEM((2, QBLK, 128), f32),
            pltpu.SemaphoreType.DMA((heads // HG + 2,)),
        ],
        cost_estimate=pl.CostEstimate(
            flops=2 * heads * QBLK * n * BLOCK * LAT, bytes_accessed=12 << 20, transcendentals=heads * QBLK * n * BLOCK
        ),
        name="teacher_terms",
        compiler_params=pltpu.CompilerParams(vmem_limit_bytes=36 << 20),
    )(*[pltpu.with_memory_space_constraint(a, pltpu.HBM) for a in (qa, qb, la, lb)], kj)


def spread_body(*refs):
    *in_refs, iq_ref, iqt_ref, wb_ref = refs
    for src in range(8):
        rows = in_refs[src][: 8 * QPART, :]
        iq_ref[src * 8 * QPART : (src + 1) * 8 * QPART, :] = rows
        iqt_ref[:, src * 8 * QPART : (src + 1) * 8 * QPART] = rows.T
        w = in_refs[src][8 * QPART :, :].astype(f32)
        for i in range(8):
            col = w[:, i : i + 1] + w[:, 8 + i : 9 + i] + w[:, 16 + i : 17 + i]
            wb_ref[src * 8 + i] = jnp.broadcast_to(col, (QPART, 128))


def spread(blocks):
    vmem = pl.BlockSpec(memory_space=pltpu.VMEM)
    return pl.pallas_call(
        spread_body,
        out_shape=(
            jax.ShapeDtypeStruct((IDXH * QPART, IDXD), bf16),
            jax.ShapeDtypeStruct((IDXD, IDXH * QPART), bf16),
            jax.ShapeDtypeStruct((IDXH, QPART, 128), f32),
        ),
        in_specs=[vmem] * 8,
        out_specs=(vmem,) * 3,
        cost_estimate=pl.CostEstimate(flops=0, bytes_accessed=3 << 20, transcendentals=0),
        name="spread",
        compiler_params=pltpu.CompilerParams(vmem_limit_bytes=8 << 20),
    )(*blocks)


PS = 4


def score_body(iq_ref, wb_ref, kj_ref, out_ref, raw_ref):
    raw = dot_nt(iq_ref[...], kj_ref[...].reshape(-1, IDXD))
    raw_ref[...] = raw.astype(bf16)
    for t in range(PS):
        acc = None
        for e in range(IDXH):
            r = raw[e * QPART : (e + 1) * QPART, t * 128 : (t + 1) * 128]
            part = jnp.maximum(r, 0.0) * wb_ref[e]
            acc = part if acc is None else acc + part
        out_ref[:, t * 128 : (t + 1) * 128] = acc


def scores(iq, wb, kj):
    n = kj.shape[0]
    return pl.pallas_call(
        score_body,
        out_shape=(
            jax.ShapeDtypeStruct((QPART, n * BLOCK), f32),
            jax.ShapeDtypeStruct((IDXH * QPART, n * BLOCK), bf16),
        ),
        grid=(n // PS,),
        in_specs=[whole(iq), whole(wb), pl.BlockSpec((PS, BLOCK, IDXD), lambda i: (i, 0, 0))],
        out_specs=(
            pl.BlockSpec((QPART, PS * BLOCK), lambda i: (0, i)),
            pl.BlockSpec((IDXH * QPART, PS * BLOCK), lambda i: (0, i)),
        ),
        cost_estimate=pl.CostEstimate(flops=2 * IDXH * QPART * n * BLOCK * IDXD, bytes_accessed=12 << 20, transcendentals=0),
        name="scores",
        compiler_params=pltpu.CompilerParams(vmem_limit_bytes=24 << 20),
    )(iq, wb, kj)


PB = 4


def backward_body(own_ref, t1_ref, t2_ref, t3_ref, score_ref, iqt_ref, wb_ref, raw_ref, kj_ref, gk_ref, *refs):
    *gq_refs, grad_ref, gr_ref, acc_ref = refs
    step = pl.program_id(0)
    span = PB * BLOCK

    @pl.when(step == 0)
    def _():
        teacher = own_ref[...] + t1_ref[...].astype(f32) + t2_ref[...].astype(f32) + t3_ref[...].astype(f32)
        target = teacher / jnp.sum(teacher, axis=1, keepdims=True)
        score = score_ref[...]
        e = jnp.exp(score - jnp.max(score, axis=1, keepdims=True))
        probs = e / jnp.sum(e, axis=1, keepdims=True)
        grad_ref[...] = loss_scale * (probs - target)
        acc_ref[...] = jnp.zeros_like(acc_ref)

    keys = kj_ref[...].reshape(-1, IDXD)
    for t in range(PB):
        g = grad_ref[:, pl.ds(pl.multiple_of(step * span + t * 128, 128), 128)]
        at = slice(t * 128, (t + 1) * 128)
        for e in range(IDXH):
            rows = slice(e * QPART, (e + 1) * QPART)
            gr_ref[rows, at] = jnp.where(raw_ref[rows, at] > 0, (g * wb_ref[e]).astype(bf16), 0)
    gr = gr_ref[...]
    gk_ref[...] = dot(iqt_ref[...], gr).T.astype(gk_ref.dtype)
    acc_ref[...] += dot(gr, keys)

    @pl.when(step == pl.num_programs(0) - 1)
    def _():
        for src in range(8):
            gq_refs[src][...] = acc_ref[src * 8 * QPART : (src + 1) * 8 * QPART, :].astype(bf16)


def backward(own, moved, score, iqt, wb, raw, kj):
    n = kj.shape[0]
    fixed = (own, *moved, score, iqt, wb)
    return pl.pallas_call(
        backward_body,
        out_shape=(
            pltpu.HBM((n * BLOCK, IDXD), bf16),
            jax.ShapeDtypeStruct((8 * QPART, IDXD), bf16),
        )
        + (pltpu.HBM((8 * QPART, IDXD), bf16),) * 7,
        grid=(n // PB,),
        in_specs=[whole(a) for a in fixed]
        + [
            pl.BlockSpec((IDXH * QPART, PB * BLOCK), lambda i: (0, i)),
            pl.BlockSpec((PB, BLOCK, IDXD), lambda i: (i, 0, 0)),
        ],
        out_specs=(pl.BlockSpec((PB * BLOCK, IDXD), lambda i: (i, 0)),)
        + (pl.BlockSpec((8 * QPART, IDXD), lambda i: (0, 0)),) * 8,
        scratch_shapes=[
            pltpu.VMEM((QPART, n * BLOCK), f32),
            pltpu.VMEM((IDXH * QPART, PB * BLOCK), bf16),
            pltpu.VMEM((IDXH * QPART, IDXD), f32),
        ],
        cost_estimate=pl.CostEstimate(flops=4 * IDXH * QPART * n * BLOCK * IDXD, bytes_accessed=16 << 20, transcendentals=0),
        name="backward",
        compiler_params=pltpu.CompilerParams(vmem_limit_bytes=30 << 20),
    )(*fixed, raw, kj)


def step(queries, lse, latent, index_keys, index_queries, index_weights, block_lists, block_place):
    head = lax.axis_index("head")
    core = head & 1
    quarter = head >> 1
    partner = [(h, h ^ 1) for h in range(8)]

    wanted = lookup(block_lists, block_place).reshape(SEL, 1, 2)
    wanted = lax.all_to_all(wanted, "seq", split_axis=0, concat_axis=0, tiled=True).reshape(SEL, 2)

    packed = pack_pages(core.reshape(1), wanted, latent.transpose(0, 2, 1), index_keys)
    kj = lax.all_to_all(packed, "seq", split_axis=0, concat_axis=0, tiled=True)

    dealt = [*deal(head.reshape(1), index_queries, index_weights.T)]
    dealt = dealt[:1] + [lax.ppermute(dealt[k], "head", [(h, (h + k) & 7) for h in range(8)]) for k in range(1, 8)]
    iq, iqt, wb = spread(dealt)

    qa, qs, la, ls = flip_queries(jnp.stack([core, quarter]), queries.transpose(1, 2, 0), lse.T)
    qb = lax.ppermute(qs, "head", partner)
    lb = lax.ppermute(ls, "head", partner)

    *parts, own = teacher_terms(qa, qb, la, lb, kj)
    moved = []
    for d in (2, 1, 3):
        ring = [(2 * x + c, 2 * ((x + d) % 4) + c) for x in range(4) for c in range(2)]
        moved.append(lax.ppermute(parts[d - 1], "head", ring))
    score, raw = scores(iq, wb, kj)

    gk, *gq = backward(own, moved, score, iqt, wb, raw, kj)

    gk = lax.all_to_all(gk.reshape(128, 16, IDXD), ("seq", "head"), split_axis=0, concat_axis=0, tiled=True)
    gq = gq[:1] + [lax.ppermute(gq[k], "head", [(h, (h - k) & 7) for h in range(8)]) for k in range(1, 8)]
    gq, gw = place(head.reshape(1), index_queries, index_weights.T, gq)
    return gq, gw.T, add_pages(wanted, gk)


def solution(mesh):
    return jax.shard_map(
        step,
        mesh=mesh,
        in_specs=(
            P("seq", "head", None),
            P("seq", "head"),
            P("seq", None, None),
            P("seq", None, None),
            P("seq", "head", None),
            P("seq", "head"),
            P("seq", None),
            P(),
        ),
        out_specs=(P("seq", "head", None), P("seq", "head"), P("seq", "head", None)),
        check_vma=False,
    )
```

```python
import math

import jax
import jax.numpy as jnp
from jax import lax
from jax.experimental import pallas as pl
from jax.experimental.pallas import tpu as pltpu
from jax.sharding import PartitionSpec as P


BLOCK = 128
SEL = 16
QBLK = 128
LAT = 576
LATP = 640
IDXD = 128
IDXH = 64
QPART = 32
ROWS = LAT + IDXD
PAGES = 64

f32 = jnp.float32
bf16 = jnp.bfloat16

LOG2E = math.log2(math.e)
softmax_scale = 192.0 ** (-0.5)
loss_scale = 2048.0


def dot(a, b):
    return lax.dot_general(a, b, (((1,), (0,)), ((), ())), preferred_element_type=f32)


def dot_nt(a, b):
    return lax.dot_general(a, b, (((1,), (1,)), ((), ())), preferred_element_type=f32)


def whole(a):
    return pl.BlockSpec(a.shape, lambda *i: (0,) * a.ndim)


def lookup_body(lists_ref, place_ref, out_ref):
    for k in range(SEL):
        for b in range(2):
            out_ref[k, b] = place_ref[lists_ref[b, k]] & (PAGES - 1)


def lookup(lists, place):
    smem = pl.BlockSpec(memory_space=pltpu.SMEM)
    return pl.pallas_call(
        lookup_body,
        out_shape=jax.ShapeDtypeStruct((SEL, 2), jnp.int32),
        in_specs=[smem, smem],
        out_specs=smem,
        name="lookup",
    )(lists, place)


def pack_body(core_ref, wanted_ref, lat_ref, key_ref, out_ref, pages, sems, done):
    reads, writes = [], []
    for i in range(SEL):
        slot = wanted_ref[i, core_ref[0]]
        reads.append(
            (
                pltpu.make_async_copy(lat_ref.at[slot], pages.at[i, pl.ds(BLOCK, LAT), :], sems.at[2 * i]),
                pltpu.make_async_copy(key_ref.at[slot], pages.at[i, pl.ds(0, BLOCK), :], sems.at[2 * i + 1]),
            )
        )
        writes.append(pltpu.make_async_copy(pages.at[i], out_ref.at[i], done.at[i]))
    for pair in reads:
        for c in pair:
            c.start()
    for pair, w in zip(reads, writes):
        for c in pair:
            c.wait()
        w.start()
    for w in writes:
        w.wait()


def pack_pages(core, wanted, lat, keys):
    return pl.pallas_call(
        pack_body,
        out_shape=jax.ShapeDtypeStruct((SEL, ROWS, BLOCK), bf16),
        in_specs=[
            pl.BlockSpec(memory_space=pltpu.SMEM),
            pl.BlockSpec(memory_space=pltpu.SMEM),
            pl.BlockSpec(memory_space=pl.ANY),
            pl.BlockSpec(memory_space=pl.ANY),
        ],
        out_specs=pl.BlockSpec(memory_space=pl.ANY),
        scratch_shapes=[
            pltpu.VMEM((SEL, ROWS, BLOCK), bf16),
            pltpu.SemaphoreType.DMA((2 * SEL,)),
            pltpu.SemaphoreType.DMA((SEL,)),
        ],
        cost_estimate=pl.CostEstimate(flops=0, bytes_accessed=6 << 20, transcendentals=0),
        name="pack_pages",
    )(core, wanted, lat, keys)


def flip_body(place_ref, qo_ref, qs_ref, lo_ref, ls_ref, own_ref, send_ref, lown_ref, lsend_ref):
    to = [pl.ds(pl.multiple_of(((k + 3 - place_ref[1]) & 3) * QPART, QPART), QPART) for k in range(4)]
    for q_ref, o_ref in ((qo_ref, own_ref), (qs_ref, send_ref)):
        for h in range(q_ref.shape[0]):
            rows = q_ref[h].T
            for k in range(4):
                o_ref[h, to[k], :LAT] = rows[k * QPART : (k + 1) * QPART]
            o_ref[h, :, LAT:] = jnp.zeros((QBLK, LATP - LAT), bf16)

    @pl.when(pl.program_id(0) == 0)
    def _():
        for l_ref, o_ref in ((lo_ref, lown_ref), (ls_ref, lsend_ref)):
            o_ref[...] = jnp.zeros_like(o_ref)
            rows = l_ref[...].T * LOG2E
            for k in range(4):
                o_ref[to[k], : l_ref.shape[0]] = rows[k * QPART : (k + 1) * QPART]


def flip_queries(place, qt, lt):
    heads = qt.shape[0]
    hb = 4
    qspec = lambda own: pl.BlockSpec((hb, LAT, QBLK), lambda i, c: (i, 0, c[0] if own else 1 - c[0]))
    lspec = lambda own: pl.BlockSpec((heads, QBLK), lambda i, c: (0, c[0] if own else 1 - c[0]))
    oq = jax.ShapeDtypeStruct((heads, QBLK, LATP), bf16)
    ol = jax.ShapeDtypeStruct((QBLK, 128), f32)
    oqs = pl.BlockSpec((hb, QBLK, LATP), lambda i, c: (i, 0, 0))
    ols = pl.BlockSpec((QBLK, 128), lambda i, c: (0, 0))
    return pl.pallas_call(
        flip_body,
        out_shape=(oq, oq, ol, ol),
        grid_spec=pltpu.PrefetchScalarGridSpec(
            num_scalar_prefetch=1,
            grid=(heads // hb,),
            in_specs=[qspec(True), qspec(False), lspec(True), lspec(False)],
            out_specs=(oqs, oqs, ols, ols),
        ),
        cost_estimate=pl.CostEstimate(flops=0, bytes_accessed=24 << 20, transcendentals=0),
        name="flip_queries",
    )(place, qt, qt, lt, lt)


def first_query(h):
    return pl.multiple_of((h & 1) * QBLK + (h >> 1) * QPART, QPART)


def deal_body(head_ref, iq_ref, w_ref, *refs):
    *out_refs, wt_ref = refs
    wt_ref[...] = w_ref[...].T
    for k in range(8):
        q0 = first_query((head_ref[0] + k) & 7)
        rows = pltpu.einshape("qed->eqd", iq_ref[pl.ds(q0, QPART)].astype(f32))
        out_refs[k][: 8 * QPART, :] = rows.reshape(8 * QPART, IDXD).astype(bf16)
        rest = wt_ref[pl.ds(q0, QPART), :]
        pieces = []
        for _ in range(3):
            piece = rest.astype(bf16).astype(f32)
            pieces.append(piece)
            rest = rest - piece
        pieces.append(jnp.zeros((QPART, IDXD - 24), f32))
        out_refs[k][8 * QPART :, :] = jnp.concatenate(pieces, axis=1).astype(bf16)


def deal(head, iq, wt):
    vmem = pl.BlockSpec(memory_space=pltpu.VMEM)
    return pl.pallas_call(
        deal_body,
        out_shape=[jax.ShapeDtypeStruct((9 * QPART, IDXD), bf16)] + [pltpu.HBM((9 * QPART, IDXD), bf16)] * 7,
        in_specs=[pl.BlockSpec(memory_space=pltpu.SMEM), vmem, vmem],
        out_specs=[vmem] * 8,
        scratch_shapes=[pltpu.VMEM((2 * QBLK, 8), f32)],
        cost_estimate=pl.CostEstimate(flops=0, bytes_accessed=2 << 20, transcendentals=0),
        name="deal",
        compiler_params=pltpu.CompilerParams(vmem_limit_bytes=4 << 20),
    )(head, iq, wt)


def place_body(head_ref, iq_ref, w_ref, *refs):
    *in_refs, gq_ref, gw_ref, wt_ref = refs
    for k in range(8):
        q0 = first_query((head_ref[0] + k) & 7)
        rows = pltpu.einshape("eqd->qed", in_refs[k][...].astype(f32).reshape(8, QPART, IDXD))
        gq_ref[pl.ds(q0, QPART)] = rows
        wt_ref[pl.ds(q0, QPART), :] = jnp.sum(rows * iq_ref[pl.ds(q0, QPART)].astype(f32), axis=2)
    gw_ref[...] = wt_ref[...].T / w_ref[...]


def place(head, iq, wt, blocks):
    vmem = pl.BlockSpec(memory_space=pltpu.VMEM)
    return pl.pallas_call(
        place_body,
        out_shape=(jax.ShapeDtypeStruct((2 * QBLK, 8, IDXD), f32), jax.ShapeDtypeStruct((8, 2 * QBLK), f32)),
        in_specs=[pl.BlockSpec(memory_space=pltpu.SMEM)] + [vmem] * 10,
        out_specs=(vmem, vmem),
        scratch_shapes=[pltpu.VMEM((2 * QBLK, 8), f32)],
        cost_estimate=pl.CostEstimate(flops=0, bytes_accessed=2 << 20, transcendentals=0),
        name="place",
        compiler_params=pltpu.CompilerParams(vmem_limit_bytes=8 << 20),
    )(head, iq, wt, *blocks)


def add_pages_body(wanted_ref, gk_ref, out_ref):
    out_ref[...] = jnp.zeros_like(out_ref)
    for i in range(SEL):
        for b in range(2):
            rows = [gk_ref[i * 8 + 2 * x + b].astype(f32) for x in range(4)]
            out_ref[wanted_ref[i, b]] += (rows[0] + rows[1]) + (rows[2] + rows[3])


def add_pages(wanted, gk):
    vmem = pl.BlockSpec(memory_space=pltpu.VMEM)
    return pl.pallas_call(
        add_pages_body,
        out_shape=jax.ShapeDtypeStruct((PAGES, 16, IDXD), f32),
        in_specs=[pl.BlockSpec(memory_space=pltpu.SMEM), vmem],
        out_specs=vmem,
        cost_estimate=pl.CostEstimate(flops=0, bytes_accessed=1 << 20, transcendentals=0),
        name="add_pages",
        compiler_params=pltpu.CompilerParams(vmem_limit_bytes=4 << 20),
    )(wanted, gk)


HG = 8
PT = 8


def teacher_body(qa_ref, qb_ref, la_ref, lb_ref, kj_ref, t1_ref, t2_ref, t3_ref, own_ref, q_ref, l_ref, sems):
    half = qa_ref.shape[0]
    copies = []
    lses = [pltpu.make_async_copy(src, l_ref.at[k], sems.at[4 + k]) for k, src in enumerate((la_ref, lb_ref))]
    for c in lses:
        c.start()
    for g in range(2 * half // HG):
        src = (qa_ref, qb_ref)[g * HG // half].at[pl.ds(g * HG % half, HG)]
        copies.append(pltpu.make_async_copy(src, q_ref.at[pl.ds(g * HG, HG)], sems.at[g]))
    for c in copies:
        c.start()
    for c in lses:
        c.wait()
    for i in range(SEL // PT):
        keys = jnp.concatenate([kj_ref[i * PT + p, BLOCK:, :] for p in range(PT)], axis=1)
        acc = None
        for g, c in enumerate(copies):
            if i == 0:
                c.wait()
            s = dot(q_ref[g * HG : (g + 1) * HG, :, :LAT].reshape(HG * QBLK, LAT), keys)
            for k in range(HG):
                side, h = g * HG // half, g * HG % half + k
                part = jnp.exp2(s[k * QBLK : (k + 1) * QBLK] * (softmax_scale * LOG2E) - l_ref[side, :, h : h + 1])
                acc = part if acc is None else acc + part
        at = slice(i * PT * BLOCK, (i + 1) * PT * BLOCK)
        for k, ref in enumerate((t1_ref, t2_ref, t3_ref, own_ref)):
            ref[:, at] = acc[k * QPART : (k + 1) * QPART].astype(ref.dtype)


def teacher_terms(qa, qb, la, lb, kj):
    n = kj.shape[0]
    vmem = pl.BlockSpec(memory_space=pltpu.VMEM)
    hbm = pl.BlockSpec(memory_space=pltpu.HBM)
    heads = 2 * qa.shape[0]
    return pl.pallas_call(
        teacher_body,
        out_shape=[jax.ShapeDtypeStruct((QPART, n * BLOCK), t) for t in (bf16, bf16, bf16, f32)],
        in_specs=[hbm, hbm, hbm, hbm, vmem],
        out_specs=[vmem] * 4,
        scratch_shapes=[
            pltpu.VMEM((heads, QBLK, LATP), bf16),
            pltpu.VMEM((2, QBLK, 128), f32),
            pltpu.SemaphoreType.DMA((heads // HG + 2,)),
        ],
        cost_estimate=pl.CostEstimate(
            flops=2 * heads * QBLK * n * BLOCK * LAT, bytes_accessed=12 << 20, transcendentals=heads * QBLK * n * BLOCK
        ),
        name="teacher_terms",
        compiler_params=pltpu.CompilerParams(vmem_limit_bytes=36 << 20),
    )(*[pltpu.with_memory_space_constraint(a, pltpu.HBM) for a in (qa, qb, la, lb)], kj)


def spread_body(*refs):
    *in_refs, iq_ref, iqt_ref, wb_ref = refs
    for src in range(8):
        rows = in_refs[src][: 8 * QPART, :]
        iq_ref[src * 8 * QPART : (src + 1) * 8 * QPART, :] = rows
        iqt_ref[:, src * 8 * QPART : (src + 1) * 8 * QPART] = rows.T
        w = in_refs[src][8 * QPART :, :].astype(f32)
        for i in range(8):
            col = w[:, i : i + 1] + w[:, 8 + i : 9 + i] + w[:, 16 + i : 17 + i]
            wb_ref[src * 8 + i] = jnp.broadcast_to(col, (QPART, 128))


def spread(blocks):
    vmem = pl.BlockSpec(memory_space=pltpu.VMEM)
    return pl.pallas_call(
        spread_body,
        out_shape=(
            jax.ShapeDtypeStruct((IDXH * QPART, IDXD), bf16),
            jax.ShapeDtypeStruct((IDXD, IDXH * QPART), bf16),
            jax.ShapeDtypeStruct((IDXH, QPART, 128), f32),
        ),
        in_specs=[vmem] * 8,
        out_specs=(vmem,) * 3,
        cost_estimate=pl.CostEstimate(flops=0, bytes_accessed=3 << 20, transcendentals=0),
        name="spread",
        compiler_params=pltpu.CompilerParams(vmem_limit_bytes=8 << 20),
    )(*blocks)


PS = 4


def score_body(iq_ref, wb_ref, kj_ref, out_ref, raw_ref):
    raw = dot_nt(iq_ref[...], kj_ref[...].reshape(-1, IDXD))
    for t in range(PS):
        raw_ref[t] = raw[:, t * 128 : (t + 1) * 128].astype(bf16)
        acc = None
        for e in range(IDXH):
            r = raw[e * QPART : (e + 1) * QPART, t * 128 : (t + 1) * 128]
            part = jnp.maximum(r, 0.0) * wb_ref[e]
            acc = part if acc is None else acc + part
        out_ref[:, t * 128 : (t + 1) * 128] = acc


def scores(iq, wb, kj):
    n = kj.shape[0]
    return pl.pallas_call(
        score_body,
        out_shape=(
            jax.ShapeDtypeStruct((QPART, n * BLOCK), f32),
            jax.ShapeDtypeStruct((n, IDXH * QPART, BLOCK), bf16),
        ),
        grid=(n // PS,),
        in_specs=[whole(iq), whole(wb), pl.BlockSpec((PS, BLOCK, IDXD), lambda i: (i, 0, 0))],
        out_specs=(
            pl.BlockSpec((QPART, PS * BLOCK), lambda i: (0, i)),
            pl.BlockSpec((PS, IDXH * QPART, BLOCK), lambda i: (i, 0, 0)),
        ),
        cost_estimate=pl.CostEstimate(flops=2 * IDXH * QPART * n * BLOCK * IDXD, bytes_accessed=12 << 20, transcendentals=0),
        name="scores",
        compiler_params=pltpu.CompilerParams(vmem_limit_bytes=24 << 20),
    )(iq, wb, kj)


PB = 4


def backward_body(own_ref, t1_ref, t2_ref, t3_ref, score_ref, iqt_ref, wb_ref, raw_ref, kj_ref, gk_ref, *refs):
    *gq_refs, grad_ref, gr_ref, acc_ref = refs
    teacher = own_ref[...] + t1_ref[...].astype(f32) + t2_ref[...].astype(f32) + t3_ref[...].astype(f32)
    target = teacher / jnp.sum(teacher, axis=1, keepdims=True)
    score = score_ref[...]
    e = jnp.exp(score - jnp.max(score, axis=1, keepdims=True))
    probs = e / jnp.sum(e, axis=1, keepdims=True)
    grad_ref[...] = loss_scale * (probs - target)

    def grad_raw(t):
        g = grad_ref[:, t * 128 : (t + 1) * 128]
        for e in range(IDXH):
            rows = slice(e * QPART, (e + 1) * QPART)
            gr_ref[t, rows, :] = jnp.where(raw_ref[t, rows, :] > 0, (g * wb_ref[e]).astype(bf16), 0)

    def products(i):
        tiles = range(i * PB, (i + 1) * PB)
        gr = jnp.concatenate([gr_ref[t] for t in tiles], axis=1)
        gk_ref[i * PB * BLOCK : (i + 1) * PB * BLOCK, :] = dot(iqt_ref[...], gr).T.astype(gk_ref.dtype)
        part = dot(gr, kj_ref[i * PB : (i + 1) * PB, :BLOCK, :].reshape(-1, IDXD))
        acc_ref[...] = part if i == 0 else acc_ref[...] + part

    steps = raw_ref.shape[0] // PB
    for i in range(steps + 1):
        if i < steps:
            for t in range(i * PB, (i + 1) * PB):
                grad_raw(t)
        if i > 0:
            products(i - 1)
    for src in range(8):
        gq_refs[src][...] = acc_ref[src * 8 * QPART : (src + 1) * 8 * QPART, :].astype(bf16)


def backward(own, moved, score, iqt, wb, raw, kj):
    n = kj.shape[0]
    vmem = pl.BlockSpec(memory_space=pltpu.VMEM)
    args = (own, *moved, score, iqt, wb, raw, kj)
    return pl.pallas_call(
        backward_body,
        out_shape=(
            pltpu.HBM((n * BLOCK, IDXD), bf16),
            jax.ShapeDtypeStruct((8 * QPART, IDXD), bf16),
        )
        + (pltpu.HBM((8 * QPART, IDXD), bf16),) * 7,
        in_specs=[vmem] * len(args),
        out_specs=(vmem,) * 9,
        scratch_shapes=[
            pltpu.VMEM((QPART, n * BLOCK), f32),
            pltpu.VMEM((n, IDXH * QPART, BLOCK), bf16),
            pltpu.VMEM((IDXH * QPART, IDXD), f32),
        ],
        cost_estimate=pl.CostEstimate(flops=4 * IDXH * QPART * n * BLOCK * IDXD, bytes_accessed=16 << 20, transcendentals=0),
        name="backward",
        compiler_params=pltpu.CompilerParams(vmem_limit_bytes=34 << 20),
    )(*args)


def step(queries, lse, latent, index_keys, index_queries, index_weights, block_lists, block_place):
    head = lax.axis_index("head")
    core = head & 1
    quarter = head >> 1
    partner = [(h, h ^ 1) for h in range(8)]

    wanted = lookup(block_lists, block_place).reshape(SEL, 1, 2)
    wanted = lax.all_to_all(wanted, "seq", split_axis=0, concat_axis=0, tiled=True).reshape(SEL, 2)

    packed = pack_pages(core.reshape(1), wanted, latent.transpose(0, 2, 1), index_keys)
    kj = lax.all_to_all(packed, "seq", split_axis=0, concat_axis=0, tiled=True)

    dealt = [*deal(head.reshape(1), index_queries, index_weights.T)]
    dealt = dealt[:1] + [lax.ppermute(dealt[k], "head", [(h, (h + k) & 7) for h in range(8)]) for k in range(1, 8)]
    iq, iqt, wb = spread(dealt)

    qa, qs, la, ls = flip_queries(jnp.stack([core, quarter]), queries.transpose(1, 2, 0), lse.T)
    qb = lax.ppermute(qs, "head", partner)
    lb = lax.ppermute(ls, "head", partner)

    *parts, own = teacher_terms(qa, qb, la, lb, kj)
    moved = []
    for d in (2, 1, 3):
        ring = [(2 * x + c, 2 * ((x + d) % 4) + c) for x in range(4) for c in range(2)]
        moved.append(lax.ppermute(parts[d - 1], "head", ring))
    score, raw = scores(iq, wb, kj)

    gk, *gq = backward(own, moved, score, iqt, wb, raw, kj)

    gk = lax.all_to_all(gk.reshape(128, 16, IDXD), ("seq", "head"), split_axis=0, concat_axis=0, tiled=True)
    gq = gq[:1] + [lax.ppermute(gq[k], "head", [(h, (h - k) & 7) for h in range(8)]) for k in range(1, 8)]
    gq, gw = place(head.reshape(1), index_queries, index_weights.T, gq)
    return gq, gw.T, add_pages(wanted, gk)


def solution(mesh):
    return jax.shard_map(
        step,
        mesh=mesh,
        in_specs=(
            P("seq", "head", None),
            P("seq", "head"),
            P("seq", None, None),
            P("seq", None, None),
            P("seq", "head", None),
            P("seq", "head"),
            P("seq", None),
            P(),
        ),
        out_specs=(P("seq", "head", None), P("seq", "head"), P("seq", "head", None)),
        check_vma=False,
    )
```

```python
import math

import jax
import jax.numpy as jnp
from jax import lax
from jax.experimental import pallas as pl
from jax.experimental.pallas import tpu as pltpu
from jax.sharding import PartitionSpec as P


BLOCK = 128
SEL = 16
QBLK = 128
LAT = 576
LATP = 640
IDXD = 128
IDXH = 64
QPART = 32
ROWS = LAT + IDXD
PAGES = 64

f32 = jnp.float32
bf16 = jnp.bfloat16

LOG2E = math.log2(math.e)
softmax_scale = 192.0 ** (-0.5)
loss_scale = 2048.0


def dot(a, b):
    return lax.dot_general(a, b, (((1,), (0,)), ((), ())), preferred_element_type=f32)


def dot_nt(a, b):
    return lax.dot_general(a, b, (((1,), (1,)), ((), ())), preferred_element_type=f32)


def whole(a):
    return pl.BlockSpec(a.shape, lambda *i: (0,) * a.ndim)


def lookup_body(lists_ref, place_ref, out_ref):
    for k in range(SEL):
        for b in range(2):
            out_ref[k, b] = place_ref[lists_ref[b, k]] & (PAGES - 1)


def lookup(lists, place):
    smem = pl.BlockSpec(memory_space=pltpu.SMEM)
    return pl.pallas_call(
        lookup_body,
        out_shape=jax.ShapeDtypeStruct((SEL, 2), jnp.int32),
        in_specs=[smem, smem],
        out_specs=smem,
        name="lookup",
    )(lists, place)


def pack_body(core_ref, wanted_ref, lat_ref, key_ref, out_ref, pages, sems, done):
    reads, writes = [], []
    for i in range(SEL):
        slot = wanted_ref[i, core_ref[0]]
        reads.append(
            (
                pltpu.make_async_copy(lat_ref.at[slot], pages.at[i, pl.ds(BLOCK, LAT), :], sems.at[2 * i]),
                pltpu.make_async_copy(key_ref.at[slot], pages.at[i, pl.ds(0, BLOCK), :], sems.at[2 * i + 1]),
            )
        )
        writes.append(pltpu.make_async_copy(pages.at[i], out_ref.at[i], done.at[i]))
    for pair in reads:
        for c in pair:
            c.start()
    for pair, w in zip(reads, writes):
        for c in pair:
            c.wait()
        w.start()
    for w in writes:
        w.wait()


def pack_pages(core, wanted, lat, keys):
    return pl.pallas_call(
        pack_body,
        out_shape=pltpu.HBM((SEL, ROWS, BLOCK), bf16),
        in_specs=[
            pl.BlockSpec(memory_space=pltpu.SMEM),
            pl.BlockSpec(memory_space=pltpu.SMEM),
            pl.BlockSpec(memory_space=pltpu.HBM),
            pl.BlockSpec(memory_space=pltpu.HBM),
        ],
        out_specs=pl.BlockSpec(memory_space=pltpu.HBM),
        scratch_shapes=[
            pltpu.VMEM((SEL, ROWS, BLOCK), bf16),
            pltpu.SemaphoreType.DMA((2 * SEL,)),
            pltpu.SemaphoreType.DMA((SEL,)),
        ],
        cost_estimate=pl.CostEstimate(flops=0, bytes_accessed=6 << 20, transcendentals=0),
        name="pack_pages",
        compiler_params=pltpu.CompilerParams(vmem_limit_bytes=5 << 20),
    )(core, wanted, *[pltpu.with_memory_space_constraint(a, pltpu.HBM) for a in (lat, keys)])


def flip_body(place_ref, qo_ref, qs_ref, lo_ref, ls_ref, own_ref, send_ref, lown_ref, lsend_ref):
    to = [pl.ds(pl.multiple_of(((k + 3 - place_ref[1]) & 3) * QPART, QPART), QPART) for k in range(4)]
    for q_ref, o_ref in ((qo_ref, own_ref), (qs_ref, send_ref)):
        for h in range(q_ref.shape[0]):
            rows = q_ref[h].T
            for k in range(4):
                o_ref[h, to[k], :LAT] = rows[k * QPART : (k + 1) * QPART]
            o_ref[h, :, LAT:] = jnp.zeros((QBLK, LATP - LAT), bf16)

    @pl.when(pl.program_id(0) == 0)
    def _():
        for l_ref, o_ref in ((lo_ref, lown_ref), (ls_ref, lsend_ref)):
            o_ref[...] = jnp.zeros_like(o_ref)
            rows = l_ref[...].T * LOG2E
            for k in range(4):
                o_ref[to[k], : l_ref.shape[0]] = rows[k * QPART : (k + 1) * QPART]


def flip_queries(place, qt, lt):
    heads = qt.shape[0]
    hb = 4
    qspec = lambda own: pl.BlockSpec((hb, LAT, QBLK), lambda i, c: (i, 0, c[0] if own else 1 - c[0]))
    lspec = lambda own: pl.BlockSpec((heads, QBLK), lambda i, c: (0, c[0] if own else 1 - c[0]))
    oq = jax.ShapeDtypeStruct((heads, QBLK, LATP), bf16)
    ol = jax.ShapeDtypeStruct((QBLK, 128), f32)
    oqs = pl.BlockSpec((hb, QBLK, LATP), lambda i, c: (i, 0, 0))
    ols = pl.BlockSpec((QBLK, 128), lambda i, c: (0, 0))
    return pl.pallas_call(
        flip_body,
        out_shape=(oq, oq, ol, ol),
        grid_spec=pltpu.PrefetchScalarGridSpec(
            num_scalar_prefetch=1,
            grid=(heads // hb,),
            in_specs=[qspec(True), qspec(False), lspec(True), lspec(False)],
            out_specs=(oqs, oqs, ols, ols),
        ),
        cost_estimate=pl.CostEstimate(flops=0, bytes_accessed=24 << 20, transcendentals=0),
        name="flip_queries",
    )(place, qt, qt, lt, lt)


def first_query(h):
    return pl.multiple_of((h & 1) * QBLK + (h >> 1) * QPART, QPART)


def deal_body(head_ref, iq_ref, w_ref, *refs):
    *out_refs, wt_ref = refs
    wt_ref[...] = w_ref[...].T
    for k in range(8):
        q0 = first_query((head_ref[0] + k) & 7)
        rows = pltpu.einshape("qed->eqd", iq_ref[pl.ds(q0, QPART)].astype(f32))
        out_refs[k][: 8 * QPART, :] = rows.reshape(8 * QPART, IDXD).astype(bf16)
        rest = wt_ref[pl.ds(q0, QPART), :]
        pieces = []
        for _ in range(3):
            piece = rest.astype(bf16).astype(f32)
            pieces.append(piece)
            rest = rest - piece
        pieces.append(jnp.zeros((QPART, IDXD - 24), f32))
        out_refs[k][8 * QPART :, :] = jnp.concatenate(pieces, axis=1).astype(bf16)


def deal(head, iq, wt):
    vmem = pl.BlockSpec(memory_space=pltpu.VMEM)
    return pl.pallas_call(
        deal_body,
        out_shape=[jax.ShapeDtypeStruct((9 * QPART, IDXD), bf16)] + [pltpu.HBM((9 * QPART, IDXD), bf16)] * 7,
        in_specs=[pl.BlockSpec(memory_space=pltpu.SMEM), vmem, vmem],
        out_specs=[vmem] * 8,
        scratch_shapes=[pltpu.VMEM((2 * QBLK, 8), f32)],
        cost_estimate=pl.CostEstimate(flops=0, bytes_accessed=2 << 20, transcendentals=0),
        name="deal",
        compiler_params=pltpu.CompilerParams(vmem_limit_bytes=4 << 20),
    )(head, iq, wt)


def place_body(head_ref, iq_ref, w_ref, *refs):
    *in_refs, gq_ref, gw_ref, wt_ref = refs
    for k in range(8):
        q0 = first_query((head_ref[0] + k) & 7)
        rows = pltpu.einshape("eqd->qed", in_refs[k][...].astype(f32).reshape(8, QPART, IDXD))
        gq_ref[pl.ds(q0, QPART)] = rows
        wt_ref[pl.ds(q0, QPART), :] = jnp.sum(rows * iq_ref[pl.ds(q0, QPART)].astype(f32), axis=2)
    gw_ref[...] = wt_ref[...].T / w_ref[...]


def place(head, iq, wt, blocks):
    vmem = pl.BlockSpec(memory_space=pltpu.VMEM)
    return pl.pallas_call(
        place_body,
        out_shape=(jax.ShapeDtypeStruct((2 * QBLK, 8, IDXD), f32), jax.ShapeDtypeStruct((8, 2 * QBLK), f32)),
        in_specs=[pl.BlockSpec(memory_space=pltpu.SMEM)] + [vmem] * 10,
        out_specs=(vmem, vmem),
        scratch_shapes=[pltpu.VMEM((2 * QBLK, 8), f32)],
        cost_estimate=pl.CostEstimate(flops=0, bytes_accessed=2 << 20, transcendentals=0),
        name="place",
        compiler_params=pltpu.CompilerParams(vmem_limit_bytes=8 << 20),
    )(head, iq, wt, *blocks)


def add_pages_body(wanted_ref, gk_ref, out_ref):
    out_ref[...] = jnp.zeros_like(out_ref)
    for i in range(SEL):
        for b in range(2):
            rows = [gk_ref[i * 8 + 2 * x + b].astype(f32) for x in range(4)]
            out_ref[wanted_ref[i, b]] += (rows[0] + rows[1]) + (rows[2] + rows[3])


def add_pages(wanted, gk):
    vmem = pl.BlockSpec(memory_space=pltpu.VMEM)
    return pl.pallas_call(
        add_pages_body,
        out_shape=jax.ShapeDtypeStruct((PAGES, 16, IDXD), f32),
        in_specs=[pl.BlockSpec(memory_space=pltpu.SMEM), vmem],
        out_specs=vmem,
        cost_estimate=pl.CostEstimate(flops=0, bytes_accessed=1 << 20, transcendentals=0),
        name="add_pages",
        compiler_params=pltpu.CompilerParams(vmem_limit_bytes=4 << 20),
    )(wanted, gk)


HG = 8
PT = 16


def teacher_body(qa_ref, qb_ref, la_ref, lb_ref, kj_ref, t1_ref, t2_ref, t3_ref, own_ref, q_ref, l_ref, sems):
    half = qa_ref.shape[0]
    copies = []
    lses = [pltpu.make_async_copy(src, l_ref.at[k], sems.at[4 + k]) for k, src in enumerate((la_ref, lb_ref))]
    for g in range(2 * half // HG):
        src = (qa_ref, qb_ref)[g * HG // half].at[pl.ds(g * HG % half, HG)]
        copies.append(pltpu.make_async_copy(src, q_ref.at[pl.ds(g * HG, HG)], sems.at[g]))
    first, *rest = copies
    for c in (first, *lses):
        c.start()
    for c in (first, *lses):
        c.wait()
    for c in rest:
        c.start()
    for i in range(SEL // PT):
        keys = jnp.concatenate([kj_ref[i * PT + p, BLOCK:, :] for p in range(PT)], axis=1)
        acc = None
        for g in range(len(copies)):
            if i == 0 and g == 1:
                for c in rest:
                    c.wait()
            s = dot(q_ref[g * HG : (g + 1) * HG, :, :LAT].reshape(HG * QBLK, LAT), keys)
            for k in range(HG):
                side, h = g * HG // half, g * HG % half + k
                part = jnp.exp2(s[k * QBLK : (k + 1) * QBLK] * (softmax_scale * LOG2E) - l_ref[side, :, h : h + 1])
                acc = part if acc is None else acc + part
        at = slice(i * PT * BLOCK, (i + 1) * PT * BLOCK)
        for k, ref in enumerate((t1_ref, t2_ref, t3_ref, own_ref)):
            ref[:, at] = acc[k * QPART : (k + 1) * QPART].astype(ref.dtype)


def teacher_terms(qa, qb, la, lb, kj):
    n = kj.shape[0]
    vmem = pl.BlockSpec(memory_space=pltpu.VMEM)
    hbm = pl.BlockSpec(memory_space=pltpu.HBM)
    heads = 2 * qa.shape[0]
    return pl.pallas_call(
        teacher_body,
        out_shape=[jax.ShapeDtypeStruct((QPART, n * BLOCK), t) for t in (bf16, bf16, bf16, f32)],
        in_specs=[hbm, hbm, hbm, hbm, vmem],
        out_specs=[vmem] * 4,
        scratch_shapes=[
            pltpu.VMEM((heads, QBLK, LATP), bf16),
            pltpu.VMEM((2, QBLK, 128), f32),
            pltpu.SemaphoreType.DMA((heads // HG + 2,)),
        ],
        cost_estimate=pl.CostEstimate(
            flops=2 * heads * QBLK * n * BLOCK * LAT, bytes_accessed=12 << 20, transcendentals=heads * QBLK * n * BLOCK
        ),
        name="teacher_terms",
        compiler_params=pltpu.CompilerParams(vmem_limit_bytes=46 << 20),
    )(*[pltpu.with_memory_space_constraint(a, pltpu.HBM) for a in (qa, qb, la, lb)], kj)


def spread_body(*refs):
    *in_refs, iq_ref, iqt_ref, wb_ref = refs
    for src in range(8):
        rows = in_refs[src][: 8 * QPART, :]
        iq_ref[src * 8 * QPART : (src + 1) * 8 * QPART, :] = rows
        iqt_ref[:, src * 8 * QPART : (src + 1) * 8 * QPART] = rows.T
        w = in_refs[src][8 * QPART :, :].astype(f32)
        for i in range(8):
            col = w[:, i : i + 1] + w[:, 8 + i : 9 + i] + w[:, 16 + i : 17 + i]
            wb_ref[src * 8 + i] = jnp.broadcast_to(col, (QPART, 128))


def spread(blocks):
    vmem = pl.BlockSpec(memory_space=pltpu.VMEM)
    return pl.pallas_call(
        spread_body,
        out_shape=(
            jax.ShapeDtypeStruct((IDXH * QPART, IDXD), bf16),
            jax.ShapeDtypeStruct((IDXD, IDXH * QPART), bf16),
            jax.ShapeDtypeStruct((IDXH, QPART, 128), f32),
        ),
        in_specs=[vmem] * 8,
        out_specs=(vmem,) * 3,
        cost_estimate=pl.CostEstimate(flops=0, bytes_accessed=3 << 20, transcendentals=0),
        name="spread",
        compiler_params=pltpu.CompilerParams(vmem_limit_bytes=8 << 20),
    )(*blocks)


PS = 4


def score_body(iq_ref, wb_ref, kj_ref, out_ref, raw_ref):
    raw = dot_nt(iq_ref[...], kj_ref[...].reshape(-1, IDXD))
    for t in range(PS):
        raw_ref[t] = raw[:, t * 128 : (t + 1) * 128].astype(bf16)
        acc = None
        for e in range(IDXH):
            r = raw[e * QPART : (e + 1) * QPART, t * 128 : (t + 1) * 128]
            part = jnp.maximum(r, 0.0) * wb_ref[e]
            acc = part if acc is None else acc + part
        out_ref[:, t * 128 : (t + 1) * 128] = acc


def scores(iq, wb, kj):
    n = kj.shape[0]
    return pl.pallas_call(
        score_body,
        out_shape=(
            jax.ShapeDtypeStruct((QPART, n * BLOCK), f32),
            jax.ShapeDtypeStruct((n, IDXH * QPART, BLOCK), bf16),
        ),
        grid=(n // PS,),
        in_specs=[whole(iq), whole(wb), pl.BlockSpec((PS, BLOCK, IDXD), lambda i: (i, 0, 0))],
        out_specs=(
            pl.BlockSpec((QPART, PS * BLOCK), lambda i: (0, i)),
            pl.BlockSpec((PS, IDXH * QPART, BLOCK), lambda i: (i, 0, 0)),
        ),
        cost_estimate=pl.CostEstimate(flops=2 * IDXH * QPART * n * BLOCK * IDXD, bytes_accessed=12 << 20, transcendentals=0),
        name="scores",
        compiler_params=pltpu.CompilerParams(vmem_limit_bytes=24 << 20),
    )(iq, wb, kj)


PB = 4
FAR = (4,)


def backward_body(own_ref, t1_ref, t2_ref, t3_ref, score_ref, iqt_ref, wb_ref, raw_ref, kj_ref, gk_ref, *refs):
    *gq_refs, grad_ref, gr_ref, acc_ref = refs
    teacher = own_ref[...] + t1_ref[...].astype(f32) + t2_ref[...].astype(f32) + t3_ref[...].astype(f32)
    target = teacher / jnp.sum(teacher, axis=1, keepdims=True)
    score = score_ref[...]
    e = jnp.exp(score - jnp.max(score, axis=1, keepdims=True))
    probs = e / jnp.sum(e, axis=1, keepdims=True)
    grad_ref[...] = loss_scale * (probs - target)

    def grad_raw(t):
        g = grad_ref[:, t * 128 : (t + 1) * 128]
        for e in range(IDXH):
            rows = slice(e * QPART, (e + 1) * QPART)
            gr_ref[t, rows, :] = jnp.where(raw_ref[t, rows, :] > 0, (g * wb_ref[e]).astype(bf16), 0)

    def products(i):
        tiles = range(i * PB, (i + 1) * PB)
        gr = jnp.concatenate([gr_ref[t] for t in tiles], axis=1)
        gk_ref[i * PB * BLOCK : (i + 1) * PB * BLOCK, :] = dot(iqt_ref[...], gr).T.astype(gk_ref.dtype)
        part = dot(gr, kj_ref[i * PB : (i + 1) * PB, :BLOCK, :].reshape(-1, IDXD))
        acc_ref[...] = part if i == 0 else acc_ref[...] + part

    steps = raw_ref.shape[0] // PB
    for i in range(steps + 1):
        if i < steps:
            for t in range(i * PB, (i + 1) * PB):
                grad_raw(t)
        if i > 0:
            products(i - 1)
    for src in range(8):
        gq_refs[src][...] = acc_ref[src * 8 * QPART : (src + 1) * 8 * QPART, :].astype(bf16)


def backward(own, moved, score, iqt, wb, raw, kj):
    n = kj.shape[0]
    vmem = pl.BlockSpec(memory_space=pltpu.VMEM)
    args = (own, *moved, score, iqt, wb, raw, kj)
    return pl.pallas_call(
        backward_body,
        out_shape=(
            pltpu.HBM((n * BLOCK, IDXD), bf16),
            jax.ShapeDtypeStruct((8 * QPART, IDXD), bf16),
        )
        + (pltpu.HBM((8 * QPART, IDXD), bf16),) * 7,
        in_specs=[vmem] * len(args),
        out_specs=(vmem,) * 9,
        scratch_shapes=[
            pltpu.VMEM((QPART, n * BLOCK), f32),
            pltpu.VMEM((n, IDXH * QPART, BLOCK), bf16),
            pltpu.VMEM((IDXH * QPART, IDXD), f32),
        ],
        cost_estimate=pl.CostEstimate(flops=4 * IDXH * QPART * n * BLOCK * IDXD, bytes_accessed=16 << 20, transcendentals=0),
        name="backward",
        compiler_params=pltpu.CompilerParams(vmem_limit_bytes=34 << 20),
    )(*args)


def step(queries, lse, latent, index_keys, index_queries, index_weights, block_lists, block_place):
    head = lax.axis_index("head")
    core = head & 1
    quarter = head >> 1
    partner = [(h, h ^ 1) for h in range(8)]

    wanted = lookup(block_lists, block_place).reshape(SEL, 1, 2)
    wanted = lax.all_to_all(wanted, "seq", split_axis=0, concat_axis=0, tiled=True).reshape(SEL, 2)

    packed = pack_pages(core.reshape(1), wanted, latent.transpose(0, 2, 1), index_keys)
    kj = lax.all_to_all(packed, "seq", split_axis=0, concat_axis=0, tiled=True)

    dealt = [*deal(head.reshape(1), index_queries, index_weights.T)]
    dealt = dealt[:1] + [lax.ppermute(dealt[k], "head", [(h, (h + k) & 7) for h in range(8)]) for k in range(1, 8)]
    iq, iqt, wb = spread(dealt)

    qa, qs, la, ls = flip_queries(jnp.stack([core, quarter]), queries.transpose(1, 2, 0), lse.T)
    qb = lax.ppermute(qs, "head", partner)
    lb = lax.ppermute(ls, "head", partner)

    *parts, own = teacher_terms(qa, qb, la, lb, kj)
    moved = []
    for d in (2, 1, 3):
        ring = [(2 * x + c, 2 * ((x + d) % 4) + c) for x in range(4) for c in range(2)]
        moved.append(lax.ppermute(parts[d - 1], "head", ring))
    score, raw = scores(iq, wb, kj)

    gk, *gq = backward(own, moved, score, iqt, wb, raw, kj)

    home = [[(h, (h - k) & 7) for h in range(8)] for k in range(8)]
    far = {k: lax.ppermute(gq[k], "head", home[k]) for k in FAR}
    gk = lax.all_to_all(gk.reshape(128, 16, IDXD), ("seq", "head"), split_axis=0, concat_axis=0, tiled=True)
    gq = gq[:1] + [far[k] if k in far else lax.ppermute(gq[k], "head", home[k]) for k in range(1, 8)]
    gq, gw = place(head.reshape(1), index_queries, index_weights.T, gq)
    return gq, gw.T, add_pages(wanted, gk)


def solution(mesh):
    return jax.shard_map(
        step,
        mesh=mesh,
        in_specs=(
            P("seq", "head", None),
            P("seq", "head"),
            P("seq", None, None),
            P("seq", None, None),
            P("seq", "head", None),
            P("seq", "head"),
            P("seq", None),
            P(),
        ),
        out_specs=(P("seq", "head", None), P("seq", "head"), P("seq", "head", None)),
        check_vma=False,
    )
```
